128 devices in a mesh: surf: 16 (over y, z), depth: 8 (over x, core).
Axes of the slice: x: 4, y: 4, z: 4, core: 2. Of those that a mesh axis runs over, the one named last changes fastest.
Arguments:
- wave_now: float32 [4, 128, 128, 128], P(None, 'surf', 'depth'), may hold values from -6 to 6
- wave_old: float32 [4, 128, 128, 128], P(None, 'surf', 'depth'), may hold values from -6 to 6
- adj_now: float32 [4, 128, 128, 128], P(None, 'surf', 'depth'), may hold values from -6 to 6
- adj_old: float32 [4, 128, 128, 128], P(None, 'surf', 'depth'), may hold values from -6 to 6
- source: float32 [4, 128, 128, 128], P(None, 'surf', 'depth'), may hold values from -24 to 24
- adj_source: float32 [4, 128, 128, 128], P(None, 'surf', 'depth'), may hold values from -24 to 24
- inv_density: float32 [125, 32768], P(None, ('surf', 'depth')), may hold values from 0.5 to 1.5
- inv_modulus: float32 [125, 32768], P(None, ('surf', 'depth')), may hold values from 0.5 to 1.5
- element_cell: int32 [128, 256], P(('surf', 'depth')), may hold values from 0 to 255, as said below
- send_elem: int32 [128, 4, 256], P(('surf', 'depth')), may hold values from 0 to 255, as said below
- send_brick: int32 [128, 4, 256], P(('surf', 'depth')), may hold values from 0 to 1023, as said below
- send_count: int32 [128, 4], P(('surf', 'depth')), may hold values from 0 to 256, as said below
Outputs:
- wave_next: float32 [4, 128, 128, 128], P(None, 'surf', 'depth')
- adj_next: float32 [4, 128, 128, 128], P(None, 'surf', 'depth')
- brick_kernel: float32 [125, 131072], P(None, ('surf', 'depth'))
The draws below stay inside these ranges and needn't reach their ends.
Inputs may be any that keep to these rules, and one draw needn't show every extreme that they name: Each row of element_cell is a permutation of the cells of one device. `send_elem`: row t of device k lists in its first send_count[k, t] slots the stored elements of device k whose blocks go to row t's device; over the four rows of a device each of its elements is listed exactly once; other slots hold 0. `send_brick`: in live slots the receiving brick within the receiving device; other slots hold 0. `send_count`: A device's counts sum to 256; rows 1 and 3 of devices with the last surf index, and rows 2 and 3 of devices with the last depth index, are empty; in every draw the device with the last surf and depth index fills row 0 with all 256 slots.
All inputs are finite; a program needn't handle non-finite values.
Results may differ from the reference program's by a relative error of at most 0.0003.
Values sent between devices are 32-bit elements; how exact they have to be, the bound alone decides.
No kernel may reach another device: no remote copies, remote signals or barrier semaphores. Data moves between devices by JAX's collectives and lax.ppermute only.
A program may use at most 128 MiB of HBM per device.

```python
import math
import jax
import jax.numpy as jnp
import numpy as np
from jax import lax

SHOTS = 4
GLL_NODES = 125
ELEM_A = 2
ELEM_C = 4
ELEM_B = 32
BRICK_DEV = 1024
ELEM_DEV = 256
ELEMS = 32768
NODES_A = 8
NODES_C = 16
NODES_B = 128
GRID_A = 128
GRID_C = 128
SLOTS = 256
BRICKS = 131072
N_SURF = 16
N_DEPTH = 8
DEVICES = 128


def route_tables(key):
    base_key = jax.random.fold_in(key, 4242)
    cut_a = jax.random.randint(jax.random.fold_in(base_key, 1), (N_SURF,), 0, ELEM_A + 1).astype(jnp.int32)
    cut_a = jnp.where(jnp.arange(N_SURF) == N_SURF - 1, ELEM_A, cut_a).astype(jnp.int32)
    cut_c = jax.random.randint(jax.random.fold_in(base_key, 2), (N_DEPTH,), 0, ELEM_C + 1).astype(jnp.int32)
    cut_c = jnp.where(jnp.arange(N_DEPTH) == N_DEPTH - 1, ELEM_C, cut_c).astype(jnp.int32)

    def one_source(source_key, device):
        subkeys = jax.random.split(source_key, 3)
        surf_index = device // N_DEPTH
        depth_index = device % N_DEPTH
        cells = jax.random.permutation(subkeys[0], ELEM_DEV).astype(jnp.int32)
        cell_a = cells // (ELEM_C * ELEM_B)
        cell_c = cells // ELEM_B % ELEM_C
        target_row = (cell_a >= cut_a[surf_index]).astype(jnp.int32) + 2 * (cell_c >= cut_c[depth_index]).astype(jnp.int32)
        stored = jnp.arange(ELEM_DEV, dtype=jnp.int32)
        ranking = jnp.argsort(target_row, stable=True)
        sorted_row = target_row[ranking]
        counts = jnp.sum((target_row[:, None] == jnp.arange(4, dtype=jnp.int32)[None, :]).astype(jnp.int32), 0)
        starts = jnp.cumsum(counts) - counts
        slot_rank = stored - starts[sorted_row]
        element_lists = jnp.zeros((4, SLOTS), jnp.int32).at[sorted_row, slot_rank].set(stored[ranking])
        bricks = jax.random.randint(subkeys[2], (4, SLOTS), 0, BRICK_DEV).astype(jnp.int32)
        live_slot = jnp.arange(SLOTS, dtype=jnp.int32)[None, :] < counts[:, None]
        bricks = jnp.where(live_slot, bricks, 0).astype(jnp.int32)
        return (cells, element_lists, bricks, counts.astype(jnp.int32))
    source_keys = jax.random.split(jax.random.fold_in(base_key, 3), DEVICES)
    return jax.vmap(one_source)(source_keys, jnp.arange(DEVICES, dtype=jnp.int32))


def draw_element_cell(key, part):
    return route_tables(key)[0]


def draw_send_elem(key, part):
    return route_tables(key)[1]


def draw_send_brick(key, part):
    return route_tables(key)[2]


def draw_send_count(key, part):
    return route_tables(key)[3]


def shard_levels(key, dims, cuts, smallest, largest):
    factor_of = 1.0
    for dim, blocks in cuts:
        heights = jax.random.uniform(jax.random.fold_in(jax.random.fold_in(key, 6), dim), (blocks,), jnp.float32, smallest / len(cuts), largest / len(cuts))
        factor_of = factor_of * jnp.repeat(jnp.exp(heights), dims[dim] // blocks).reshape((-1,) + (1,) * (len(dims) - 1 - dim))
    return factor_of


def gaussian(rng, dims, width, limit, cuts=(), kind=jnp.bfloat16):
    result = width * jax.random.normal(rng, dims, jnp.float32)
    if cuts:
        result = result * shard_levels(rng, dims, cuts, -0.22, 0.18)
    return jnp.clip(result, -limit, limit).astype(kind)


def setup_inputs(seed: int = 0) -> dict:
    arg_keys = jax.random.split(jax.random.key(seed), 13)
    wave_now = gaussian(arg_keys[0], (SHOTS, GRID_A, GRID_C, NODES_B), 1.0, 6.0, ((1, 16), (2, 8)), jnp.float32)
    wave_old = gaussian(arg_keys[1], (SHOTS, GRID_A, GRID_C, NODES_B), 1.0, 6.0, ((1, 16), (2, 8)), jnp.float32)
    adj_now = gaussian(arg_keys[2], (SHOTS, GRID_A, GRID_C, NODES_B), 1.0, 6.0, ((1, 16), (2, 8)), jnp.float32)
    adj_old = gaussian(arg_keys[3], (SHOTS, GRID_A, GRID_C, NODES_B), 1.0, 6.0, ((1, 16), (2, 8)), jnp.float32)
    source = gaussian(arg_keys[4], (SHOTS, GRID_A, GRID_C, NODES_B), 4.0, 24.0, ((1, 16), (2, 8)), jnp.float32)
    adj_source = gaussian(arg_keys[5], (SHOTS, GRID_A, GRID_C, NODES_B), 4.0, 24.0, ((1, 16), (2, 8)), jnp.float32)
    inv_density = jnp.clip(jnp.exp(math.log(1.5) - 1.0986123 * jax.random.uniform(arg_keys[6], (GLL_NODES, ELEMS), jnp.float32) ** shard_levels(arg_keys[6], (GLL_NODES, ELEMS), ((1, 128),), -0.2, 0.2)), 0.5, 1.5)
    inv_modulus = jnp.clip(jnp.exp(math.log(1.5) - 1.0986123 * jax.random.uniform(arg_keys[7], (GLL_NODES, ELEMS), jnp.float32) ** shard_levels(arg_keys[7], (GLL_NODES, ELEMS), ((1, 128),), -0.2, 0.2)), 0.5, 1.5)
    element_cell = draw_element_cell(jax.random.fold_in(arg_keys[12], 71), 0)
    send_elem = draw_send_elem(jax.random.fold_in(arg_keys[12], 71), 0)
    send_brick = draw_send_brick(jax.random.fold_in(arg_keys[12], 71), 0)
    send_count = draw_send_count(jax.random.fold_in(arg_keys[12], 71), 0)
    return {"wave_now": wave_now, "wave_old": wave_old, "adj_now": adj_now, "adj_old": adj_old, "source": source, "adj_source": adj_source, "inv_density": inv_density, "inv_modulus": inv_modulus, "element_cell": element_cell, "send_elem": send_elem, "send_brick": send_brick, "send_count": send_count}


time_step = 0.05
precise = lax.Precision.HIGHEST

def gll_tables():
    points = np.array([-1.0, -math.sqrt(3.0 / 7.0), 0.0, math.sqrt(3.0 / 7.0), 1.0])
    weights = np.array([0.1, 49.0 / 90.0, 32.0 / 45.0, 49.0 / 90.0, 0.1])
    identity = np.eye(5)
    on_diagonal = identity > 0.5
    differences = points[:, None] - points[None, :] + identity
    products = np.prod(differences, axis=1)
    derivative = products[:, None] / products[None, :] / differences
    inverse = np.where(on_diagonal, 0.0, 1.0 / differences)
    derivative = np.where(on_diagonal, inverse.sum(axis=1)[:, None], derivative)
    return (jnp.asarray(derivative, jnp.float32), jnp.asarray(weights, jnp.float32))

def node_ids(cell_ids):
    cell_a = cell_ids // (ELEM_C * ELEM_B)
    cell_c = cell_ids // ELEM_B % ELEM_C
    cell_b = cell_ids % ELEM_B
    local_ids = jnp.arange(GLL_NODES, dtype=jnp.int32)
    along_a = local_ids // 25
    along_c = local_ids // 5 % 5
    along_b = local_ids % 5
    node_a = 4 * cell_a[None, :] + along_a[:, None]
    node_c = 4 * cell_c[None, :] + along_c[:, None]
    node_b = (4 * cell_b[None, :] + along_b[:, None]) % (4 * ELEM_B)
    return ((node_a * (4 * ELEM_C + 1) + node_c) * (4 * ELEM_B) + node_b).astype(jnp.int32)

def element_terms(values, density, modulus, shot_count):
    derivative, weights = gll_tables()
    cubature = weights[:, None, None] * weights[None, :, None] * weights[None, None, :]
    elem_count = values.shape[-1]
    nodal = values.reshape(values.shape[0], 5, 5, 5, elem_count)
    grad_a = jnp.einsum('ip,xpqre->xiqre', derivative, nodal, precision=precise)
    grad_c = jnp.einsum('jq,xpqre->xpjre', derivative, nodal, precision=precise)
    grad_b = jnp.einsum('kr,xpqre->xpqke', derivative, nodal, precision=precise)
    stiffness = cubature[..., None] * density.reshape(5, 5, 5, elem_count)
    forces = jnp.einsum('ip,xiqre->xpqre', derivative, stiffness * grad_a, precision=precise) + jnp.einsum('jq,xpjre->xpqre', derivative, stiffness * grad_c, precision=precise) + jnp.einsum('kr,xpqke->xpqre', derivative, stiffness * grad_b, precision=precise)
    lumped_mass = cubature[..., None] * modulus.reshape(5, 5, 5, elem_count)
    product = grad_a[:shot_count] * grad_a[shot_count:] + grad_c[:shot_count] * grad_c[shot_count:] + grad_b[:shot_count] * grad_b[shot_count:]
    kernel = -time_step * cubature[..., None] * lax.optimization_barrier(jnp.sum(product, axis=0))
    partial_value = jnp.concatenate([forces.reshape(2 * shot_count, GLL_NODES, elem_count), lumped_mass.reshape(1, GLL_NODES, elem_count)], 0)
    return (partial_value, kernel.reshape(GLL_NODES, elem_count))

def reference(wave_now, wave_old, adj_now, adj_old, source, adj_source, inv_density, inv_modulus, element_cell, send_elem, send_brick, send_count):
    fields = jnp.concatenate([wave_now, adj_now], 0)
    padded = jnp.pad(fields, ((0, 0), (0, 1), (0, 1), (0, 0)))
    channels = 2 * SHOTS + 1
    global_sum = jnp.zeros((channels, GRID_A + 1, GRID_C + 1, NODES_B), jnp.float32)

    def one_device(global_sum, device):
        surf_index = device // N_DEPTH
        depth_index = device % N_DEPTH
        start_a = (surf_index * NODES_A).astype(jnp.int32)
        start_c = (depth_index * NODES_C).astype(jnp.int32)
        zero_index = jnp.zeros((), jnp.int32)
        corner = (zero_index, start_a, start_c, zero_index)
        block = lax.dynamic_slice(padded, corner, (2 * SHOTS, NODES_A + 1, NODES_C + 1, NODES_B))
        flattened = block.reshape(2 * SHOTS, -1)
        cell_ids = lax.dynamic_index_in_dim(element_cell, device, 0, keepdims=False)
        node_map = node_ids(cell_ids)
        values = jnp.take(flattened, node_map, axis=1)
        column = (device * ELEM_DEV).astype(jnp.int32)
        density = lax.dynamic_slice_in_dim(inv_density, column, ELEM_DEV, 1)
        modulus = lax.dynamic_slice_in_dim(inv_modulus, column, ELEM_DEV, 1)
        partial_value, kernel = element_terms(values, density, modulus, SHOTS)
        assembled_local = jnp.zeros((channels, flattened.shape[1]), jnp.float32)
        assembled_local = assembled_local.at[:, node_map.reshape(-1)].add(partial_value.reshape(channels, -1))
        assembled_local = assembled_local.reshape(channels, NODES_A + 1, NODES_C + 1, NODES_B)
        current = lax.dynamic_slice(global_sum, corner, assembled_local.shape)
        global_sum = lax.dynamic_update_slice(global_sum, current + assembled_local, corner)
        return (global_sum, kernel)
    global_sum, kernels = lax.scan(one_device, global_sum, jnp.arange(DEVICES, dtype=jnp.int32))
    assembled = global_sum[:, :GRID_A, :GRID_C, :]
    lumped_mass = assembled[2 * SHOTS:]
    step_square = time_step * time_step
    wave_next = 2.0 * wave_now - wave_old + step_square * (source - assembled[:SHOTS]) / lumped_mass
    adj_next = 2.0 * adj_now - adj_old + step_square * (adj_source - assembled[SHOTS:2 * SHOTS]) / lumped_mass
    kernel_all = kernels.transpose(1, 0, 2).reshape(GLL_NODES, ELEMS)
    slot_ids = jnp.arange(SLOTS, dtype=jnp.int32)
    live_slot = slot_ids[None, None, :] < send_count[:, :, None]
    source_dev = jnp.arange(DEVICES, dtype=jnp.int32)[:, None, None]
    row_ids = jnp.arange(4, dtype=jnp.int32)[None, :, None]
    target_dev = ((source_dev // N_DEPTH + row_ids % 2) * N_DEPTH + source_dev % N_DEPTH + row_ids // 2).astype(jnp.int32)
    element_id = (source_dev * ELEM_DEV + send_elem).astype(jnp.int32)
    brick_id = jnp.where(live_slot, target_dev * BRICK_DEV + send_brick, -1).astype(jnp.int32)
    brick_of = jnp.full((ELEMS,), -1, jnp.int32).at[element_id.reshape(-1)].max(brick_id.reshape(-1))
    brick_kernel = jax.ops.segment_sum(kernel_all.T, brick_of, num_segments=BRICKS).T
    return (wave_next, adj_next, brick_kernel)
```

```python
import math

import jax
import jax.numpy as jnp
import numpy as np
from jax import lax
from jax.experimental import pallas as pl
from jax.experimental.pallas import tpu as pltpu
from jax.sharding import PartitionSpec as P

F32 = jnp.float32
BF16 = jnp.bfloat16
DT = 0.05
NT = (((1,), (1,)), ((), ()))
NROW = 85


def gll():
    x = np.array([-1.0, -math.sqrt(3.0 / 7.0), 0.0, math.sqrt(3.0 / 7.0), 1.0])
    w = np.array([0.1, 49.0 / 90.0, 32.0 / 45.0, 49.0 / 90.0, 0.1])
    eye = np.eye(5)
    diff = x[:, None] - x[None, :] + eye
    prod = np.prod(diff, axis=1)
    deriv = prod[:, None] / prod[None, :] / diff
    inv = np.where(eye > 0.5, 0.0, 1.0 / diff)
    deriv = np.where(eye > 0.5, inv.sum(axis=1)[:, None], deriv)
    return deriv, w


DERIV, WEIGHT = gll()
CUBATURE = (WEIGHT[:, None, None] * WEIGHT[None, :, None] * WEIGHT[None, None, :]).reshape(125, 1)


def spread_table():
    table = np.zeros((4, 128, 5, 4, 32), np.float32)
    for ec in range(4):
        for eb in range(32):
            for r in range(5):
                table[ec, (4 * eb + r) % 128, r, ec, eb] = 1.0
    return table.reshape(512, 640)


def apply_deriv(mat, v):
    e0, e1, e2 = v[0] + v[4], v[1] + v[3], v[2]
    o0, o1 = v[0] - v[4], v[1] - v[3]
    half = lambda i, l: float(0.5 * (mat[i, l] + mat[i, 4 - l]))
    dif = lambda i, l: float(0.5 * (mat[i, l] - mat[i, 4 - l]))
    odd = [half(i, 0) * e0 + half(i, 1) * e1 + float(mat[i, 2]) * e2 for i in (0, 1)]
    even = [dif(i, 0) * o0 + dif(i, 1) * o1 for i in (0, 1, 2)]
    return [even[0] + odd[0], even[1] + odd[1], even[2], even[1] - odd[1], even[0] - odd[0]]


def split2(x):
    hi = x.astype(BF16)
    return hi, (x - hi.astype(F32)).astype(BF16)


def dot2(x, table, dims=(((1,), (0,)), ((), ()))):
    hi, lo = split2(x)
    return lax.dot_general(hi, table, dims, preferred_element_type=F32) + lax.dot_general(
        lo, table, dims, preferred_element_type=F32
    )


def prep_kernel(dens, modu, cell, selem, sbrick, scount, cub, fold, stiff, mass, targ, ms0, ms1, mo):
    place = (lax.broadcasted_iota(jnp.int32, (256, 256), 0) == cell[...]).astype(F32).astype(BF16)
    stiff[0:125, :] = dot2(dens[...], place, NT) * cub[...]
    cells = dot2(modu[...], place, NT) * cub[...]
    mass[...] = jnp.zeros(mass.shape, F32)
    for ea, ms in ((0, ms0), (1, ms1)):
        ms[0:125, :] = cells[:, ea * 128 : ea * 128 + 128]
        rows = jnp.concatenate([ms[pl.ds(r, 25, stride=5), :] for r in range(5)], axis=1)
        mo[...] = dot2(rows, fold[...])
        for p in range(5):
            for ec in range(4):
                at = pl.ds((4 * ea + p) * 17 + 4 * ec, 5)
                mass[at, :] = mass[at, :] + mo[p * 5 : p * 5 + 5, ec * 128 : ec * 128 + 128]
    sub = lax.broadcasted_iota(jnp.int32, (8, 256), 0)
    lane = lax.broadcasted_iota(jnp.int32, (1, 256), 1)
    elem_iota = lax.broadcasted_iota(jnp.int32, (256, 256), 0)
    acc = jnp.zeros((8, 256), F32)
    for t in range(4):
        brick = jnp.where(lane < scount[0, t], sbrick[0, t : t + 1, :] + 1, 0)
        high = lax.shift_right_logical(brick, 5)
        low = brick - high * 32
        rows = jnp.where(sub == t, high, jnp.where(sub == t + 4, low, 0))
        pick = (elem_iota == selem[0, t : t + 1, :]).astype(F32).astype(BF16)
        acc = acc + lax.dot_general(
            rows.astype(F32).astype(BF16), pick, NT, preferred_element_type=F32
        )
    at_cell = lax.dot_general(acc.astype(BF16), place, NT, preferred_element_type=F32)
    targ[0:4, :] = 32.0 * at_cell[0:4] + at_cell[4:8] - 1.0


def element_layer(ea, stiff, spread, fold, kcol, kern, ng, g, lhs, val, prod, frc):
    for p in range(5):
        for c in range(17):
            tile = g[pl.ds(p * 17 + c, 8, stride=NROW), :]
            if c < 16:
                at = (p * 5 + c % 4) * 8
                lhs[at : at + 8, (c // 4) * 128 : (c // 4) * 128 + 128] = tile
            if c % 4 == 0 and c > 0:
                at = (p * 5 + 4) * 8
                lhs[at : at + 8, (c // 4 - 1) * 128 : (c // 4 - 1) * 128 + 128] = tile
    val[...] = dot2(lhs[...], spread[...])

    def tile_at(p, q, r):
        return (slice((p * 5 + q) * 8, (p * 5 + q) * 8 + 8), slice(r * 128, r * 128 + 128))

    lanes = slice(ea * 128, ea * 128 + 128)
    prod[1000:1024, :] = jnp.zeros((24, 128), F32)
    for axis in range(3):
        for i in range(5):
            for j in range(5):
                nodes = [((k, i, j), (i, k, j), (i, j, k))[axis] for k in range(5)]
                grad = apply_deriv(DERIV, [val[tile_at(*n)] for n in nodes])
                flux = []
                for k, n in enumerate(nodes):
                    at = n[0] * 25 + n[1] * 5 + n[2]
                    flux.append(grad[k] * stiff[at : at + 1, lanes])
                force = apply_deriv(DERIV.T, flux)
                for k, n in enumerate(nodes):
                    at = (n[0] * 25 + n[1] * 5 + n[2]) * 8
                    pair = grad[k] * pltpu.roll(grad[k], 4, 0)
                    if axis == 0:
                        prod[at : at + 8, :] = pair
                        frc[tile_at(*n)] = force[k]
                    else:
                        prod[at : at + 8, :] = prod[at : at + 8, :] + pair
                        frc[tile_at(*n)] = frc[tile_at(*n)] + force[k]
    for j in range(16):
        total = sum(prod[pl.ds(j * 64 + t, 8, stride=8), :] for t in range(4))
        kern[j * 8 : j * 8 + 8, :] = total * kcol[j * 8 : j * 8 + 8, :]
    lhs[...] = dot2(frc[...], fold[...])
    for p in range(5):
        for c in range(17):
            parts = []
            if c < 16:
                at = (p * 5 + c % 4) * 8
                parts.append(lhs[at : at + 8, (c // 4) * 128 : (c // 4) * 128 + 128])
            if c % 4 == 0 and c > 0:
                at = (p * 5 + 4) * 8
                parts.append(lhs[at : at + 8, (c // 4 - 1) * 128 : (c // 4 - 1) * 128 + 128])
            ng[pl.ds(p * 17 + c, 8, stride=NROW), :] = sum(parts)


def low_kernel(wave, adj, hc, stiff, spread, fold, kcol, kern, ng, g, lhs, val, prod, frc):
    keep = (lax.axis_index("depth") < lax.axis_size("depth") - 1).astype(F32)
    for x in range(8):
        src = wave if x < 4 else adj
        for p in range(5):
            at = x * NROW + p * 17
            g[at : at + 16, :] = src[x % 4, p]
            g[at + 16 : at + 17, :] = hc[x, p : p + 1, :] * keep
    element_layer(0, stiff, spread, fold, kcol, kern, ng, g, lhs, val, prod, frc)


def high_kernel(
    wave, adj, hc, ha, stiff, spread, fold, kcol, kern_low, ng_low, mass, targ,
    inner, own, buf_s, buf_d, buf_sd, kern, ng, g, lhs, val, prod, frc,
):
    keep_d = (lax.axis_index("depth") < lax.axis_size("depth") - 1).astype(F32)
    keep_s = (lax.axis_index("surf") < lax.axis_size("surf") - 1).astype(F32)
    for x in range(8):
        src = wave if x < 4 else adj
        for p in range(4):
            at = x * NROW + p * 17
            g[at : at + 16, :] = src[x % 4, 4 + p]
            g[at + 16 : at + 17, :] = hc[x, 4 + p : 5 + p, :] * keep_d
        at = x * NROW + 68
        g[at : at + 16, :] = ha[x, 0:16, :] * keep_s
        g[at + 16 : at + 17, :] = ha[x, 16:17, :] * (keep_s * keep_d)
    element_layer(1, stiff, spread, fold, kcol, kern, ng, g, lhs, val, prod, frc)
    for row, buf in ((0, own), (1, buf_s), (2, buf_d), (3, buf_sd)):
        buf[0:128, :] = kern_low[...]
        buf[128:256, :] = kern[...]
        buf[125:126, :] = targ[row : row + 1, 0:128]
        buf[253:254, :] = targ[row : row + 1, 128:256]
    for x in range(8):
        base = x * NROW
        for a in range(8):
            if a < 4:
                rows = ng_low[base + a * 17 : base + a * 17 + 17, :]
            elif a == 4:
                rows = ng_low[base + 68 : base + 85, :] + ng[base : base + 17, :]
            else:
                at = base + (a - 4) * 17
                rows = ng[at : at + 17, :]
            inner[x, a] = rows[0:16]
            buf_d[256 + x * 8 + a : 257 + x * 8 + a, :] = rows[16:17]
        buf_s[256 + x * 16 : 272 + x * 16, :] = ng[base + 68 : base + 84, :]
        buf_sd[256 + x : 257 + x, :] = ng[base + 84 : base + 85, :]
    for a in range(8):
        inner[8, a] = mass[a * 17 : a * 17 + 16, :]
        buf_d[320 + a : 321 + a, :] = mass[a * 17 + 16 : a * 17 + 17, :]
    buf_s[384:400, :] = mass[136:152, :]
    buf_sd[264:265, :] = mass[152:153, :]
    buf_sd[265:272, :] = jnp.zeros((7, 128), F32)


def final_kernel(
    wave, wave_old, adj, adj_old, src, adj_src, inner, own, got_s, got_d, got_sd,
    wave_next, adj_next, bricks,
):
    has_s = lax.axis_index("surf") > 0
    has_d = lax.axis_index("depth") > 0
    keep_s = has_s.astype(F32)
    keep_d = has_d.astype(F32)
    first = lax.broadcasted_iota(jnp.int32, (16, 128), 0) == 0

    def total(ch, a):
        part = inner[ch, a]
        line = got_d[256 + ch * 8 + a : 257 + ch * 8 + a, :] * keep_d
        if a == 0:
            part = part + got_s[256 + ch * 16 : 272 + ch * 16, :] * keep_s
            line = line + got_sd[256 + ch : 257 + ch, :] * (keep_s * keep_d)
        return part + jnp.where(first, line, 0.0)

    for a in range(8):
        scale = (DT * DT) / total(8, a)
        for t in range(4):
            wave_next[t, a] = 2.0 * wave[t, a] - wave_old[t, a] + (src[t, a] - total(t, a)) * scale
            adj_next[t, a] = (
                2.0 * adj[t, a] - adj_old[t, a] + (adj_src[t, a] - total(4 + t, a)) * scale
            )
    rows = lax.broadcasted_iota(jnp.int32, (1024, 128), 0).astype(F32)
    acc = jnp.zeros((128, 1024), F32)
    for buf in (own, got_s, got_d, got_sd):
        for ea in range(2):
            block = buf[ea * 128 : ea * 128 + 128, :]
            hit = jnp.where(rows == block[125:126, :], 1.0, 0.0).astype(BF16)
            acc = acc + dot2(block, hit, NT)
    bricks[...] = acc[0:125, :]


def vmem(*shape):
    return pltpu.VMEM(shape, F32)


def out(*shape):
    return jax.ShapeDtypeStruct(shape, F32)


PARAMS = pltpu.CompilerParams(vmem_limit_bytes=48 * 1024 * 1024)


def ring(x, axis, by):
    size = lax.axis_size(axis)
    return lax.ppermute(x, axis, [(i, (i + by) % size) for i in range(size)])


def diagonal(x):
    ns, nd = lax.axis_size("surf"), lax.axis_size("depth")
    pairs = [
        (s * nd + d, (s + 1) % ns * nd + (d + 1) % nd) for s in range(ns) for d in range(nd)
    ]
    return lax.ppermute(x, ("surf", "depth"), pairs)


def per_device(
    wave_now, wave_old, adj_now, adj_old, source, adj_source,
    inv_density, inv_modulus, element_cell, send_elem, send_brick, send_count,
):
    table = spread_table()
    spread = jnp.asarray(table, BF16)
    fold = jnp.asarray(table.T, BF16)
    cub = jnp.asarray(CUBATURE, F32)
    kcol = jnp.asarray(np.concatenate([-DT * CUBATURE, np.zeros((3, 1))]), F32)

    hc = ring(jnp.concatenate([wave_now[:, :, 0], adj_now[:, :, 0]], 0), "depth", -1)
    plane = jnp.concatenate([wave_now[:, 0], adj_now[:, 0]], 0)
    ha = ring(jnp.concatenate([plane, hc[:, 0:1]], 1), "surf", -1)

    any_ = pl.BlockSpec(memory_space=pltpu.VMEM)
    smem = pl.BlockSpec(memory_space=pltpu.SMEM)
    stiff, mass, targ = pl.pallas_call(
        prep_kernel,
        out_shape=(out(128, 256), out(160, 128), out(8, 256)),
        in_specs=[any_] * 5 + [smem] + [any_] * 2,
        out_specs=(any_, any_, any_),
        scratch_shapes=[vmem(128, 128), vmem(128, 128), vmem(25, 512)],
        compiler_params=PARAMS,
        name="prep",
    )(inv_density, inv_modulus, element_cell, send_elem, send_brick, send_count, cub, fold)

    work = [vmem(8 * NROW, 128), vmem(200, 512), vmem(200, 640), vmem(1024, 128), vmem(200, 640)]
    kern_low, ng_low = pl.pallas_call(
        low_kernel,
        out_shape=(out(128, 128), out(8 * NROW, 128)),
        in_specs=[any_] * 7,
        out_specs=(any_, any_),
        scratch_shapes=work,
        compiler_params=PARAMS,
        name="low",
    )(wave_now, adj_now, hc, stiff, spread, fold, kcol)

    inner, own, buf_s, buf_d, buf_sd = pl.pallas_call(
        high_kernel,
        out_shape=(out(9, 8, 16, 128), out(256, 128), out(400, 128), out(328, 128), out(272, 128)),
        in_specs=[any_] * 12,
        out_specs=(any_,) * 5,
        scratch_shapes=[vmem(128, 128), vmem(8 * NROW, 128)] + work,
        compiler_params=PARAMS,
        name="high",
    )(wave_now, adj_now, hc, ha, stiff, spread, fold, kcol, kern_low, ng_low, mass, targ)

    got_s = ring(buf_s, "surf", 1)
    got_d = ring(buf_d, "depth", 1)
    got_sd = diagonal(buf_sd)

    field = out(*wave_now.shape)
    return pl.pallas_call(
        final_kernel,
        out_shape=(field, field, out(125, 1024)),
        in_specs=[any_] * 11,
        out_specs=(any_,) * 3,
        compiler_params=PARAMS,
        name="final",
    )(
        wave_now, wave_old, adj_now, adj_old, source, adj_source, inner, own, got_s, got_d, got_sd
    )


def solution(mesh):
    field = P(None, "surf", "depth", None)
    both = ("surf", "depth")
    return jax.shard_map(
        per_device,
        mesh=mesh,
        in_specs=(field,) * 6
        + (P(None, both), P(None, both), P(both, None), P(both, None, None), P(both, None, None), P(both, None)),
        out_specs=(field, field, P(None, both)),
        check_vma=False,
    )
```

```python
import math

import jax
import jax.numpy as jnp
import numpy as np
from jax import lax
from jax.experimental import pallas as pl
from jax.experimental.pallas import tpu as pltpu
from jax.sharding import PartitionSpec as P

F32 = jnp.float32
BF16 = jnp.bfloat16
DT = 0.05
NT = (((1,), (1,)), ((), ()))
NROW = 85
PLANE = 128


def gll():
    x = np.array([-1.0, -math.sqrt(3.0 / 7.0), 0.0, math.sqrt(3.0 / 7.0), 1.0])
    w = np.array([0.1, 49.0 / 90.0, 32.0 / 45.0, 49.0 / 90.0, 0.1])
    eye = np.eye(5)
    diff = x[:, None] - x[None, :] + eye
    prod = np.prod(diff, axis=1)
    deriv = prod[:, None] / prod[None, :] / diff
    inv = np.where(eye > 0.5, 0.0, 1.0 / diff)
    deriv = np.where(eye > 0.5, inv.sum(axis=1)[:, None], deriv)
    return deriv, w


DERIV, WEIGHT = gll()


def apply_deriv(mat, v):
    e0, e1, e2 = v[0] + v[4], v[1] + v[3], v[2]
    o0, o1 = v[0] - v[4], v[1] - v[3]
    half = lambda i, l: float(0.5 * (mat[i, l] + mat[i, 4 - l]))
    dif = lambda i, l: float(0.5 * (mat[i, l] - mat[i, 4 - l]))
    odd = [half(i, 0) * e0 + half(i, 1) * e1 + float(mat[i, 2]) * e2 for i in (0, 1)]
    even = [dif(i, 0) * o0 + dif(i, 1) * o1 for i in (0, 1, 2)]
    return [even[0] + odd[0], even[1] + odd[1], even[2], even[1] - odd[1], even[0] - odd[0]]


def split2(x):
    hi = x.astype(BF16)
    return hi, (x - hi.astype(F32)).astype(BF16)


def dot2(x, table, dims=(((1,), (0,)), ((), ()))):
    hi, lo = split2(x)
    return lax.dot_general(hi, table, dims, preferred_element_type=F32) + lax.dot_general(
        lo, table, dims, preferred_element_type=F32
    )


def pack_kernel(wave, adj, line, plane, sem):
    copies = []
    for k, src in enumerate((wave, adj)):
        to = pl.ds(4 * k, 4)
        copies.append(pltpu.make_async_copy(src.at[:, :, 0, :], line.at[to], sem.at[2 * k]))
        copies.append(pltpu.make_async_copy(src.at[:, 0], plane.at[to], sem.at[2 * k + 1]))
    for c in copies:
        c.start()
    for c in copies:
        c.wait()


def prep_kernel(
    dens_hbm, modu_hbm, cell_hbm, selem_hbm, sbrick_hbm, scount, stiff, mass, targ, spread, fold, wcol,
    dens, modu, cell, selem, sbrick, sem, ms0, ms1, mo,
):
    pairs = (
        (dens_hbm, dens), (modu_hbm, modu), (cell_hbm, cell), (selem_hbm, selem), (sbrick_hbm, sbrick)
    )
    copies = [pltpu.make_async_copy(a, b, sem.at[k]) for k, (a, b) in enumerate(pairs)]
    for c in copies:
        c.start()
    sub = lax.broadcasted_iota(jnp.int32, (128, 128), 0)
    lane = lax.broadcasted_iota(jnp.int32, (128, 128), 1)
    fold[...] = jnp.zeros(fold.shape, BF16)
    for r in range(5):
        node = (4 * (lane & 31) + r) & 127
        hit = sub == node
        for ec in range(4):
            spread[ec * 128 : ec * 128 + 128, r * 128 : r * 128 + 128] = jnp.where(
                hit & ((lane >> 5) == ec), 1.0, 0.0
            ).astype(BF16)
        back = jnp.where(lane == ((4 * (sub & 31) + r) & 127), 1.0, 0.0).astype(BF16)
        for ec in range(4):
            rows = slice(r * 128 + ec * 32, r * 128 + ec * 32 + 32)
            fold[rows, ec * 128 : ec * 128 + 128] = back[ec * 32 : ec * 32 + 32]

    def weight(i):
        edge = float(WEIGHT[0])
        return jnp.where(
            i == 2, float(WEIGHT[2]), jnp.where((i == 0) | (i == 4), edge, float(WEIGHT[1]))
        )

    p = (sub >= 25).astype(jnp.int32) + (sub >= 50) + (sub >= 75) + (sub >= 100) + (sub >= 125)
    rest = sub - 25 * p
    q = (rest >= 5).astype(jnp.int32) + (rest >= 10) + (rest >= 15) + (rest >= 20)
    cub = weight(p) * weight(q) * weight(rest - 5 * q)
    wcol[...] = cub * -DT
    for c in copies:
        c.wait()
    both = jnp.concatenate([cub[0:125], cub[0:125]], axis=1)
    place = (lax.broadcasted_iota(jnp.int32, (256, 256), 0) == cell[...]).astype(F32).astype(BF16)
    stiff[0:125, :] = dot2(dens[...], place, NT) * both
    cells = dot2(modu[...], place, NT) * both
    mass[...] = jnp.zeros(mass.shape, F32)
    for ea, ms in ((0, ms0), (1, ms1)):
        ms[0:125, :] = cells[:, ea * 128 : ea * 128 + 128]
        rows = jnp.concatenate([ms[pl.ds(r, 25, stride=5), :] for r in range(5)], axis=1)
        mo[...] = dot2(rows, fold[...])
        for p in range(5):
            for ec in range(4):
                at = pl.ds((4 * ea + p) * 17 + 4 * ec, 5)
                mass[at, :] = mass[at, :] + mo[p * 5 : p * 5 + 5, ec * 128 : ec * 128 + 128]
    sub = lax.broadcasted_iota(jnp.int32, (8, 256), 0)
    lane = lax.broadcasted_iota(jnp.int32, (1, 256), 1)
    elem_iota = lax.broadcasted_iota(jnp.int32, (256, 256), 0)
    acc = jnp.zeros((8, 256), F32)
    for t in range(4):
        brick = jnp.where(lane < scount[0, t], sbrick[0, t : t + 1, :] + 1, 0)
        high = lax.shift_right_logical(brick, 5)
        low = brick - high * 32
        rows = jnp.where(sub == t, high, jnp.where(sub == t + 4, low, 0))
        pick = (elem_iota == selem[0, t : t + 1, :]).astype(F32).astype(BF16)
        acc = acc + lax.dot_general(
            rows.astype(F32).astype(BF16), pick, NT, preferred_element_type=F32
        )
    at_cell = lax.dot_general(acc.astype(BF16), place, NT, preferred_element_type=F32)
    targ[0:4, :] = 32.0 * at_cell[0:4] + at_cell[4:8] - 1.0


def load_plane(g, step, p, lhs, row):
    for c in range(17):
        tile = g[pl.ds(p * 17 + c, 8, stride=step), :]
        if c < 16:
            at = row + c % 4 * 8
            lhs[at : at + 8, c // 4 * 128 : c // 4 * 128 + 128] = tile
        if c % 4 == 0 and c > 0:
            lhs[row + 32 : row + 40, (c // 4 - 1) * 128 : c // 4 * 128] = tile


def node_tile(p, q, r):
    return (slice((p * 5 + q) * 8, (p * 5 + q) * 8 + 8), slice(r * 128, r * 128 + 128))


def node_rows(p, q, r):
    at = (p * 25 + q * 5 + r) * 8
    return slice(at, at + 8)


def line_terms(ea, nodes, values, stiff):
    lanes = slice(ea * 128, ea * 128 + 128)
    grad = apply_deriv(DERIV, values)
    flux = []
    for k, (p, q, r) in enumerate(nodes):
        at = p * 25 + q * 5 + r
        flux.append(grad[k] * stiff[at : at + 1, lanes])
    return [g * pltpu.roll(g, 4, 0) for g in grad], apply_deriv(DERIV.T, flux)


def inside_plane(ea, p, val, at, stiff, prod, frc):
    for i in range(5):
        nodes = [(p, k, i) for k in range(5)]
        pair, force = line_terms(ea, nodes, [val[node_tile(at, k, i)] for k in range(5)], stiff)
        for k, n in enumerate(nodes):
            prod[node_rows(*n), :] = pair[k]
            frc[node_tile(*n)] = force[k]
    for i in range(5):
        nodes = [(p, i, k) for k in range(5)]
        pair, force = line_terms(ea, nodes, [val[node_tile(at, i, k)] for k in range(5)], stiff)
        for k, n in enumerate(nodes):
            prod[node_rows(*n), :] = prod[node_rows(*n), :] + pair[k]
            frc[node_tile(*n)] = frc[node_tile(*n)] + force[k]


def across_planes(ea, val, last, stiff, prod_in, frc_in, prod, frc):
    for q in range(5):
        for r in range(5):
            nodes = [(k, q, r) for k in range(5)]
            values = [val[node_tile(k, q, r)] for k in range(4)] + [last(q, r)]
            pair, force = line_terms(ea, nodes, values, stiff)
            for k, n in enumerate(nodes):
                old_p, old_f = (prod_in, frc_in) if k < 4 else (prod, frc)
                prod[node_rows(*n), :] = old_p[node_rows(*n), :] + pair[k]
                frc[node_tile(*n)] = old_f[node_tile(*n)] + force[k]


def finish_layer(prod, frc, lhs, fold, wcol, kern, ng):
    for j in range(16):
        count = 8 if j < 15 else 5
        total = sum(prod[pl.ds(j * 64 + t, count, stride=8), :] for t in range(4))
        kern[j * 8 : j * 8 + count, :] = total * wcol[j * 8 : j * 8 + count, :]
    kern[125:128, :] = jnp.zeros((3, 128), F32)
    lhs[...] = dot2(frc[...], fold[...])
    for p in range(5):
        for c in range(17):
            parts = []
            if c < 16:
                at = (p * 5 + c % 4) * 8
                parts.append(lhs[at : at + 8, c // 4 * 128 : c // 4 * 128 + 128])
            if c % 4 == 0 and c > 0:
                at = (p * 5 + 4) * 8
                parts.append(lhs[at : at + 8, (c // 4 - 1) * 128 : c // 4 * 128])
            ng[pl.ds(p * 17 + c, 8, stride=NROW), :] = sum(parts)


def early_kernel(
    wave, adj, hc, stiff, spread, fold, wcol, kern, ng, val_up, prod_up, frc_up, g, lhs, val, prod, frc
):
    keep = (lax.axis_index("depth") < lax.axis_size("depth") - 1).astype(F32)
    for ea, planes in ((0, 5), (1, 4)):
        for x in range(8):
            src = wave if x < 4 else adj
            for p in range(planes):
                at = x * NROW + p * 17
                row = x % 4 * PLANE + (4 * ea + p) * 16
                g[at : at + 16, :] = src[row : row + 16, :]
                g[at + 16 : at + 17, :] = hc[x, 4 * ea + p : 4 * ea + p + 1, :] * keep
        for p in range(planes):
            load_plane(g, NROW, p, lhs, p * 40)
        if ea == 0:
            val[...] = dot2(lhs[...], spread[...])
            for p in range(5):
                inside_plane(0, p, val, p, stiff, prod, frc)
            across_planes(0, val, lambda q, r: val[node_tile(4, q, r)], stiff, prod, frc, prod, frc)
            finish_layer(prod, frc, lhs, fold, wcol, kern, ng)
        else:
            val_up[...] = dot2(lhs[0:160, :], spread[...])
            for p in range(4):
                inside_plane(1, p, val_up, p, stiff, prod_up, frc_up)


def late_kernel(
    ha, stiff, spread, fold, wcol, kern_low, ng_low, mass, targ, val_up, prod_up, frc_up,
    inner, own, buf_s, buf_d, buf_sd, kern, ng, g, lhs, val, prod, frc,
):
    keep_d = (lax.axis_index("depth") < lax.axis_size("depth") - 1).astype(F32)
    keep_s = (lax.axis_index("surf") < lax.axis_size("surf") - 1).astype(F32)
    for x in range(8):
        g[x * 17 : x * 17 + 16, :] = ha[x, 0:16, :] * keep_s
        g[x * 17 + 16 : x * 17 + 17, :] = ha[x, 16:17, :] * (keep_s * keep_d)
    load_plane(g, 17, 0, lhs, 0)
    val[...] = dot2(lhs[0:40, :], spread[...])
    inside_plane(1, 4, val, 0, stiff, prod, frc)
    across_planes(1, val_up, lambda q, r: val[node_tile(0, q, r)], stiff, prod_up, frc_up, prod, frc)
    finish_layer(prod, frc, lhs, fold, wcol, kern, ng)
    for row, buf in ((0, own), (1, buf_s), (2, buf_d), (3, buf_sd)):
        buf[0:128, :] = kern_low[...]
        buf[128:256, :] = kern[...]
        buf[125:126, :] = targ[row : row + 1, 0:128]
        buf[253:254, :] = targ[row : row + 1, 128:256]
    for x in range(8):
        base = x * NROW
        for a in range(8):
            if a < 4:
                rows = ng_low[base + a * 17 : base + a * 17 + 17, :]
            elif a == 4:
                rows = ng_low[base + 68 : base + 85, :] + ng[base : base + 17, :]
            else:
                at = base + (a - 4) * 17
                rows = ng[at : at + 17, :]
            inner[x, a] = rows[0:16]
            buf_d[256 + x * 8 + a : 257 + x * 8 + a, :] = rows[16:17]
        buf_s[256 + x * 16 : 272 + x * 16, :] = ng[base + 68 : base + 84, :]
        buf_sd[256 + x : 257 + x, :] = ng[base + 84 : base + 85, :]
    for a in range(8):
        inner[8, a] = mass[a * 17 : a * 17 + 16, :]
        buf_d[320 + a : 321 + a, :] = mass[a * 17 + 16 : a * 17 + 17, :]
    buf_s[384:400, :] = mass[136:152, :]
    buf_sd[264:265, :] = mass[152:153, :]
    buf_sd[265:272, :] = jnp.zeros((7, 128), F32)


def add_bricks(acc, buf, rows):
    for ea in range(2):
        block = buf[ea * 128 : ea * 128 + 128, :]
        hit = jnp.where(rows == block[125:126, :], 1.0, 0.0).astype(BF16)
        term = dot2(block, hit, NT)
        acc = term if acc is None else acc + term
    return acc


def own_kernel(own, part):
    rows = lax.broadcasted_iota(jnp.int32, (1024, 128), 0).astype(F32)
    part[...] = add_bricks(None, own, rows)


def final_kernel(
    wave, wave_old, adj, adj_old, src, adj_src, inner, part, got_s, got_d, got_sd,
    wave_next, adj_next, bricks, wave_buf, adj_buf, brick_buf, sem,
):
    has_s = lax.axis_index("surf") > 0
    has_d = lax.axis_index("depth") > 0
    keep_s = has_s.astype(F32)
    keep_d = has_d.astype(F32)
    first = lax.broadcasted_iota(jnp.int32, (16, 128), 0) == 0

    def total(ch, a):
        part = inner[ch, a]
        line = got_d[256 + ch * 8 + a : 257 + ch * 8 + a, :] * keep_d
        if a == 0:
            part = part + got_s[256 + ch * 16 : 272 + ch * 16, :] * keep_s
            line = line + got_sd[256 + ch : 257 + ch, :] * (keep_s * keep_d)
        return part + jnp.where(first, line, 0.0)

    for a in range(8):
        scale = (DT * DT) / total(8, a)
        for t in range(4):
            at = slice(t * PLANE + a * 16, t * PLANE + a * 16 + 16)
            wave_buf[at, :] = 2.0 * wave[at, :] - wave_old[at, :] + (src[at, :] - total(t, a)) * scale
            adj_buf[at, :] = (
                2.0 * adj[at, :] - adj_old[at, :] + (adj_src[at, :] - total(4 + t, a)) * scale
            )
    copies = [
        pltpu.make_async_copy(wave_buf, wave_next, sem.at[0]),
        pltpu.make_async_copy(adj_buf, adj_next, sem.at[1]),
    ]
    for c in copies:
        c.start()
    for k in range(2):
        cols = slice(k * 512, k * 512 + 512)
        rows = lax.broadcasted_iota(jnp.int32, (512, 128), 0).astype(F32) + float(k * 512)
        acc = part[:, cols]
        for buf in (got_s, got_d, got_sd):
            acc = add_bricks(acc, buf, rows)
        brick_buf[:, cols] = acc[0:125, :]
        copy = pltpu.make_async_copy(brick_buf.at[:, cols], bricks.at[:, cols], sem.at[2 + k])
        copy.start()
        copies.append(copy)
    for c in copies:
        c.wait()


def vmem(*shape):
    return pltpu.VMEM(shape, F32)


def out(*shape, dtype=F32):
    return jax.ShapeDtypeStruct(shape, dtype)


def send(x, ds, dd, wrap_s, wrap_d):
    ns, nd = lax.axis_size("surf"), lax.axis_size("depth")
    pairs = [
        (s * nd + d, (s + ds) % ns * nd + (d + dd) % nd)
        for s in range(ns)
        for d in range(nd)
        if (wrap_s or 0 <= s + ds < ns) and (wrap_d or 0 <= d + dd < nd)
    ]
    return lax.ppermute(x, ("surf", "depth"), pairs)


def call(kernel, name, ins, outs, scratch=(), specs=None, out_space=pltpu.VMEM):
    here = pl.BlockSpec(memory_space=pltpu.VMEM)
    return pl.pallas_call(
        kernel,
        out_shape=tuple(outs),
        in_specs=specs or [here] * len(ins),
        out_specs=tuple(pl.BlockSpec(memory_space=out_space) for _ in outs),
        scratch_shapes=list(scratch),
        compiler_params=pltpu.CompilerParams(vmem_limit_bytes=48 * 1024 * 1024),
        name=name,
    )(*ins)


def in_hbm(x):
    return pltpu.with_memory_space_constraint(x, pltpu.HBM)


def per_device(
    wave_now, wave_old, adj_now, adj_old, source, adj_source,
    inv_density, inv_modulus, element_cell, send_elem, send_brick, send_count,
):
    shape = wave_now.shape
    wave, wave_old, adj, adj_old, source, adj_source = (
        x.reshape(4 * PLANE, 128)
        for x in (wave_now, wave_old, adj_now, adj_old, source, adj_source)
    )
    there = pl.BlockSpec(memory_space=pltpu.HBM)
    line, plane = call(
        pack_kernel, "pack", [in_hbm(x) for x in (wave_now, adj_now)], (out(8, 8, 128), out(8, 16, 128)),
        [pltpu.SemaphoreType.DMA((4,))], [there] * 2,
    )
    hc = send(line, 0, -1, True, True)
    prep = call(
        prep_kernel,
        "prep",
        [in_hbm(x) for x in (inv_density, inv_modulus, element_cell, send_elem, send_brick)]
        + [send_count],
        (out(128, 256), out(160, 128), out(8, 256), out(512, 640, dtype=BF16),
         out(640, 512, dtype=BF16), out(128, 128)),
        [vmem(125, 256), vmem(125, 256), pltpu.VMEM((1, 256), jnp.int32),
         pltpu.VMEM((1, 4, 256), jnp.int32), pltpu.VMEM((1, 4, 256), jnp.int32),
         pltpu.SemaphoreType.DMA((5,)), vmem(128, 128), vmem(128, 128), vmem(25, 512)],
        [there] * 5 + [pl.BlockSpec(memory_space=pltpu.SMEM)],
    )
    hc, plane, prep = lax.optimization_barrier((hc, plane, tuple(prep)))
    stiff, mass, targ, spread, fold, wcol = prep
    ha = send(jnp.concatenate([plane, hc[:, 0:1]], 1), -1, 0, True, True)

    kern_low, ng_low, val_up, prod_up, frc_up = call(
        early_kernel,
        "early",
        (wave, adj, hc, stiff, spread, fold, wcol),
        (out(128, 128), out(8 * NROW, 128), out(160, 640), out(800, 128), out(160, 640)),
        [vmem(8 * NROW, 128), vmem(200, 512), vmem(200, 640), vmem(1000, 128), vmem(200, 640)],
    )
    inner, own, buf_s, buf_d, buf_sd = call(
        late_kernel,
        "late",
        (ha, stiff, spread, fold, wcol, kern_low, ng_low, mass, targ, val_up, prod_up, frc_up),
        (out(9, 8, 16, 128), out(256, 128), out(400, 128), out(328, 128), out(272, 128)),
        [vmem(128, 128), vmem(8 * NROW, 128), vmem(8 * 17, 128), vmem(200, 512), vmem(40, 640),
         vmem(1000, 128), vmem(200, 640)],
    )
    got_s = send(buf_s, 1, 0, False, True)
    got_d = send(buf_d, 0, 1, True, True)
    got_sd = send(buf_sd, 1, 1, False, False)
    (part,) = call(own_kernel, "own", (own,), (out(128, 1024),))
    wave_next, adj_next, bricks = call(
        final_kernel,
        "final",
        (wave, wave_old, adj, adj_old, source, adj_source, inner, part, got_s, got_d, got_sd),
        (out(4 * PLANE, 128), out(4 * PLANE, 128), out(125, 1024)),
        [vmem(4 * PLANE, 128), vmem(4 * PLANE, 128), vmem(125, 1024), pltpu.SemaphoreType.DMA((4,))],
        out_space=pl.ANY,
    )
    return wave_next.reshape(shape), adj_next.reshape(shape), bricks


def solution(mesh):
    field = P(None, "surf", "depth", None)
    both = ("surf", "depth")
    return jax.shard_map(
        per_device,
        mesh=mesh,
        in_specs=(field,) * 6
        + (P(None, both), P(None, both), P(both, None), P(both, None, None), P(both, None, None), P(both, None)),
        out_specs=(field, field, P(None, both)),
        check_vma=False,
    )
```

```python
import math

import jax
import jax.numpy as jnp
import numpy as np
from jax import lax
from jax.experimental import pallas as pl
from jax.experimental.pallas import tpu as pltpu
from jax.sharding import PartitionSpec as P

F32 = jnp.float32
BF16 = jnp.bfloat16
DT = 0.05
NT = (((1,), (1,)), ((), ()))
CHUNKS = 2
NROW = 85
PLANE = 128


def gll():
    x = np.array([-1.0, -math.sqrt(3.0 / 7.0), 0.0, math.sqrt(3.0 / 7.0), 1.0])
    w = np.array([0.1, 49.0 / 90.0, 32.0 / 45.0, 49.0 / 90.0, 0.1])
    eye = np.eye(5)
    diff = x[:, None] - x[None, :] + eye
    prod = np.prod(diff, axis=1)
    deriv = prod[:, None] / prod[None, :] / diff
    inv = np.where(eye > 0.5, 0.0, 1.0 / diff)
    deriv = np.where(eye > 0.5, inv.sum(axis=1)[:, None], deriv)
    return deriv, w


DERIV, WEIGHT = gll()


def apply_deriv(mat, v):
    e0, e1, e2 = v[0] + v[4], v[1] + v[3], v[2]
    o0, o1 = v[0] - v[4], v[1] - v[3]
    half = lambda i, l: float(0.5 * (mat[i, l] + mat[i, 4 - l]))
    dif = lambda i, l: float(0.5 * (mat[i, l] - mat[i, 4 - l]))
    odd = [half(i, 0) * e0 + half(i, 1) * e1 + float(mat[i, 2]) * e2 for i in (0, 1)]
    even = [dif(i, 0) * o0 + dif(i, 1) * o1 for i in (0, 1, 2)]
    return [even[0] + odd[0], even[1] + odd[1], even[2], even[1] - odd[1], even[0] - odd[0]]


def split2(x):
    hi = x.astype(BF16)
    return hi, (x - hi.astype(F32)).astype(BF16)


def dot2(x, table, dims=(((1,), (0,)), ((), ()))):
    hi, lo = split2(x)
    return lax.dot_general(hi, table, dims, preferred_element_type=F32) + lax.dot_general(
        lo, table, dims, preferred_element_type=F32
    )


def pack_kernel(wave, adj, line, plane, sem):
    copies = []
    for k, src in enumerate((wave, adj)):
        to = pl.ds(4 * k, 4)
        copies.append(pltpu.make_async_copy(src.at[:, :, 0, :], line.at[to], sem.at[2 * k]))
        copies.append(pltpu.make_async_copy(src.at[:, 0], plane.at[to], sem.at[2 * k + 1]))
    for c in copies:
        c.start()
    for c in copies:
        c.wait()


def prep_kernel(
    dens_hbm, modu_hbm, cell_hbm, selem_hbm, sbrick_hbm, scount, stiff, mass, targ, spread, fold, wcol,
    dens, modu, cell, selem, sbrick, sem, ms0, ms1, mo,
):
    pairs = (
        (dens_hbm, dens), (modu_hbm, modu), (cell_hbm, cell), (selem_hbm, selem), (sbrick_hbm, sbrick)
    )
    copies = [pltpu.make_async_copy(a, b, sem.at[k]) for k, (a, b) in enumerate(pairs)]
    for c in copies:
        c.start()
    sub = lax.broadcasted_iota(jnp.int32, (128, 128), 0)
    lane = lax.broadcasted_iota(jnp.int32, (128, 128), 1)
    fold[...] = jnp.zeros(fold.shape, BF16)
    for r in range(5):
        node = (4 * (lane & 31) + r) & 127
        hit = sub == node
        for ec in range(4):
            spread[ec * 128 : ec * 128 + 128, r * 128 : r * 128 + 128] = jnp.where(
                hit & ((lane >> 5) == ec), 1.0, 0.0
            ).astype(BF16)
        back = jnp.where(lane == ((4 * (sub & 31) + r) & 127), 1.0, 0.0).astype(BF16)
        for ec in range(4):
            rows = slice(r * 128 + ec * 32, r * 128 + ec * 32 + 32)
            fold[rows, ec * 128 : ec * 128 + 128] = back[ec * 32 : ec * 32 + 32]

    def weight(i):
        edge = float(WEIGHT[0])
        return jnp.where(
            i == 2, float(WEIGHT[2]), jnp.where((i == 0) | (i == 4), edge, float(WEIGHT[1]))
        )

    p = (sub >= 25).astype(jnp.int32) + (sub >= 50) + (sub >= 75) + (sub >= 100) + (sub >= 125)
    rest = sub - 25 * p
    q = (rest >= 5).astype(jnp.int32) + (rest >= 10) + (rest >= 15) + (rest >= 20)
    cub = weight(p) * weight(q) * weight(rest - 5 * q)
    wcol[...] = cub * -DT
    for c in copies:
        c.wait()
    both = jnp.concatenate([cub[0:125], cub[0:125]], axis=1)
    place = (lax.broadcasted_iota(jnp.int32, (256, 256), 0) == cell[...]).astype(F32).astype(BF16)
    stiff[0:125, :] = dot2(dens[...], place, NT) * both
    cells = dot2(modu[...], place, NT) * both
    mass[...] = jnp.zeros(mass.shape, F32)
    for ea, ms in ((0, ms0), (1, ms1)):
        ms[0:125, :] = cells[:, ea * 128 : ea * 128 + 128]
        rows = jnp.concatenate([ms[pl.ds(r, 25, stride=5), :] for r in range(5)], axis=1)
        mo[...] = dot2(rows, fold[...])
        for p in range(5):
            for ec in range(4):
                at = pl.ds((4 * ea + p) * 17 + 4 * ec, 5)
                mass[at, :] = mass[at, :] + mo[p * 5 : p * 5 + 5, ec * 128 : ec * 128 + 128]
    sub = lax.broadcasted_iota(jnp.int32, (8, 256), 0)
    lane = lax.broadcasted_iota(jnp.int32, (1, 256), 1)
    elem_iota = lax.broadcasted_iota(jnp.int32, (256, 256), 0)
    acc = jnp.zeros((8, 256), F32)
    for t in range(4):
        brick = jnp.where(lane < scount[0, t], sbrick[0, t : t + 1, :] + 1, 0)
        high = lax.shift_right_logical(brick, 5)
        low = brick - high * 32
        rows = jnp.where(sub == t, high, jnp.where(sub == t + 4, low, 0))
        pick = (elem_iota == selem[0, t : t + 1, :]).astype(F32).astype(BF16)
        acc = acc + lax.dot_general(
            rows.astype(F32).astype(BF16), pick, NT, preferred_element_type=F32
        )
    at_cell = lax.dot_general(acc.astype(BF16), place, NT, preferred_element_type=F32)
    targ[0:4, :] = 32.0 * at_cell[0:4] + at_cell[4:8] - 1.0


def load_plane(g, step, p, lhs, row):
    for c in range(17):
        tile = g[pl.ds(p * 17 + c, 8, stride=step), :]
        if c < 16:
            at = row + c % 4 * 8
            lhs[at : at + 8, c // 4 * 128 : c // 4 * 128 + 128] = tile
        if c % 4 == 0 and c > 0:
            lhs[row + 32 : row + 40, (c // 4 - 1) * 128 : c // 4 * 128] = tile


def node_tile(p, q, r):
    return (slice((p * 5 + q) * 8, (p * 5 + q) * 8 + 8), slice(r * 128, r * 128 + 128))


def node_rows(p, q, r):
    at = (p * 25 + q * 5 + r) * 8
    return slice(at, at + 8)


def line_terms(ea, nodes, values, stiff):
    lanes = slice(ea * 128, ea * 128 + 128)
    grad = apply_deriv(DERIV, values)
    flux = []
    for k, (p, q, r) in enumerate(nodes):
        at = p * 25 + q * 5 + r
        flux.append(grad[k] * stiff[at : at + 1, lanes])
    return [g * pltpu.roll(g, 4, 0) for g in grad], apply_deriv(DERIV.T, flux)


def inside_plane(ea, p, val, at, stiff, prod, frc):
    for i in range(5):
        nodes = [(p, k, i) for k in range(5)]
        pair, force = line_terms(ea, nodes, [val[node_tile(at, k, i)] for k in range(5)], stiff)
        for k, n in enumerate(nodes):
            prod[node_rows(*n), :] = pair[k]
            frc[node_tile(*n)] = force[k]
    for i in range(5):
        nodes = [(p, i, k) for k in range(5)]
        pair, force = line_terms(ea, nodes, [val[node_tile(at, i, k)] for k in range(5)], stiff)
        for k, n in enumerate(nodes):
            prod[node_rows(*n), :] = prod[node_rows(*n), :] + pair[k]
            frc[node_tile(*n)] = frc[node_tile(*n)] + force[k]


def across_planes(ea, val, last, stiff, prod_in, frc_in, prod, frc):
    for q in range(5):
        for r in range(5):
            nodes = [(k, q, r) for k in range(5)]
            values = [val[node_tile(k, q, r)] for k in range(4)] + [last(q, r)]
            pair, force = line_terms(ea, nodes, values, stiff)
            for k, n in enumerate(nodes):
                old_p, old_f = (prod_in, frc_in) if k < 4 else (prod, frc)
                prod[node_rows(*n), :] = old_p[node_rows(*n), :] + pair[k]
                frc[node_tile(*n)] = old_f[node_tile(*n)] + force[k]


def finish_layer(prod, frc, lhs, fold, wcol, kern, ng):
    for j in range(16):
        count = 8 if j < 15 else 5
        total = sum(prod[pl.ds(j * 64 + t, count, stride=8), :] for t in range(4))
        kern[j * 8 : j * 8 + count, :] = total * wcol[j * 8 : j * 8 + count, :]
    kern[125:128, :] = jnp.zeros((3, 128), F32)
    lhs[...] = dot2(frc[...], fold[...])
    for p in range(5):
        for c in range(17):
            parts = []
            if c < 16:
                at = (p * 5 + c % 4) * 8
                parts.append(lhs[at : at + 8, c // 4 * 128 : c // 4 * 128 + 128])
            if c % 4 == 0 and c > 0:
                at = (p * 5 + 4) * 8
                parts.append(lhs[at : at + 8, (c // 4 - 1) * 128 : c // 4 * 128])
            ng[pl.ds(p * 17 + c, 8, stride=NROW), :] = sum(parts)


def early_kernel(
    wave, adj, hc, stiff, spread, fold, wcol, kern, ng, val_up, prod_up, frc_up, g, lhs, val, prod, frc
):
    keep = (lax.axis_index("depth") < lax.axis_size("depth") - 1).astype(F32)
    for ea, planes in ((0, 5), (1, 4)):
        for x in range(8):
            src = wave if x < 4 else adj
            for p in range(planes):
                at = x * NROW + p * 17
                row = x % 4 * PLANE + (4 * ea + p) * 16
                g[at : at + 16, :] = src[row : row + 16, :]
                g[at + 16 : at + 17, :] = hc[x, 4 * ea + p : 4 * ea + p + 1, :] * keep
        for p in range(planes):
            load_plane(g, NROW, p, lhs, p * 40)
        if ea == 0:
            val[...] = dot2(lhs[...], spread[...])
            for p in range(5):
                inside_plane(0, p, val, p, stiff, prod, frc)
            across_planes(0, val, lambda q, r: val[node_tile(4, q, r)], stiff, prod, frc, prod, frc)
            finish_layer(prod, frc, lhs, fold, wcol, kern, ng)
        else:
            val_up[...] = dot2(lhs[0:160, :], spread[...])
            for p in range(4):
                inside_plane(1, p, val_up, p, stiff, prod_up, frc_up)


def late_kernel(
    ha, stiff, spread, fold, wcol, kern_low, ng_low, mass, targ, val_up, prod_up, frc_up,
    ng, own, buf_s, buf_d, buf_sd, kern, g, lhs, val, prod, frc,
):
    keep_d = (lax.axis_index("depth") < lax.axis_size("depth") - 1).astype(F32)
    keep_s = (lax.axis_index("surf") < lax.axis_size("surf") - 1).astype(F32)
    for x in range(8):
        g[x * 17 : x * 17 + 16, :] = ha[x * 16 : x * 16 + 16, :] * keep_s
        g[x * 17 + 16 : x * 17 + 17, :] = ha[128 + x : 129 + x, :] * (keep_s * keep_d)
    load_plane(g, 17, 0, lhs, 0)
    val[...] = dot2(lhs[0:40, :], spread[...])
    inside_plane(1, 4, val, 0, stiff, prod, frc)
    across_planes(1, val_up, lambda q, r: val[node_tile(0, q, r)], stiff, prod_up, frc_up, prod, frc)
    finish_layer(prod, frc, lhs, fold, wcol, kern, ng)
    for row, buf in ((0, own), (1, buf_s), (2, buf_d), (3, buf_sd)):
        buf[0:128, :] = kern_low[...]
        buf[128:256, :] = kern[...]
        buf[125:126, :] = targ[row : row + 1, 0:128]
        buf[253:254, :] = targ[row : row + 1, 128:256]
    for x in range(8):
        base = x * NROW
        for a in range(8):
            at = base + a * 17 + 16
            if a < 4:
                row = ng_low[at : at + 1, :]
            elif a == 4:
                row = ng_low[at : at + 1, :] + ng[base + 16 : base + 17, :]
            else:
                row = ng[at - 68 : at - 67, :]
            buf_d[256 + x * 8 + a : 257 + x * 8 + a, :] = row
        buf_s[256 + x * 16 : 272 + x * 16, :] = ng[base + 68 : base + 84, :]
        buf_sd[256 + x : 257 + x, :] = ng[base + 84 : base + 85, :]
    for a in range(8):
        buf_d[320 + a : 321 + a, :] = mass[a * 17 + 16 : a * 17 + 17, :]
    buf_s[384:400, :] = mass[136:152, :]
    buf_sd[264:265, :] = mass[152:153, :]
    buf_sd[265:272, :] = jnp.zeros((7, 128), F32)


def add_bricks(acc, buf, first=0, count=1024):
    bricks = lax.broadcasted_iota(jnp.int32, (count, 128), 0).astype(F32) + float(first)
    for ea in range(2):
        block = buf[ea * 128 : ea * 128 + 128, :]
        hit = jnp.where(bricks == block[125:126, :], 1.0, 0.0).astype(BF16)
        term = dot2(block, hit, NT)
        acc = term if acc is None else acc + term
    return acc


def near_kernel(own, got_d, ng_low, ng, mass, near, inner):
    near[...] = add_bricks(add_bricks(None, own), got_d)
    for x in range(8):
        for a in range(8):
            low, high = x * NROW + a * 17, x * NROW + (a - 4) * 17
            if a < 4:
                inner[x, a] = ng_low[low : low + 16, :]
            elif a == 4:
                inner[x, a] = ng_low[low : low + 16, :] + ng[high : high + 16, :]
            else:
                inner[x, a] = ng[high : high + 16, :]
    for a in range(8):
        inner[8, a] = mass[a * 17 : a * 17 + 16, :]


def final_kernel(
    wave, wave_old, adj, adj_old, src, adj_src, inner, near, got_s, got_d, got_sd,
    wave_next, adj_next, bricks, wave_buf, adj_buf, brick_buf, sem,
):
    keep_s = (lax.axis_index("surf") > 0).astype(F32)
    keep_d = (lax.axis_index("depth") > 0).astype(F32)
    first = lax.broadcasted_iota(jnp.int32, (16, 128), 0) == 0

    def total(ch, a):
        part = inner[ch, a]
        line = got_d[256 + ch * 8 + a : 257 + ch * 8 + a, :] * keep_d
        if a == 0:
            part = part + got_s[256 + ch * 16 : 272 + ch * 16, :] * keep_s
            line = line + got_sd[256 + ch : 257 + ch, :] * (keep_s * keep_d)
        return part + jnp.where(first, line, 0.0)

    for a in range(8):
        scale = (DT * DT) / total(8, a)
        for t in range(4):
            at = slice(t * PLANE + a * 16, t * PLANE + a * 16 + 16)
            wave_buf[at, :] = 2.0 * wave[at, :] - wave_old[at, :] + (src[at, :] - total(t, a)) * scale
            adj_buf[at, :] = (
                2.0 * adj[at, :] - adj_old[at, :] + (adj_src[at, :] - total(4 + t, a)) * scale
            )
    copies = [
        pltpu.make_async_copy(wave_buf, wave_next, sem.at[0]),
        pltpu.make_async_copy(adj_buf, adj_next, sem.at[1]),
    ]
    for c in copies:
        c.start()
    for k in range(CHUNKS):
        cols = slice(k * (1024 // CHUNKS), (k + 1) * (1024 // CHUNKS))
        acc = near[:, cols]
        for buf in (got_s, got_sd):
            acc = add_bricks(acc, buf, k * (1024 // CHUNKS), 1024 // CHUNKS)
        brick_buf[:, cols] = acc[0:125, :]
        copy = pltpu.make_async_copy(brick_buf.at[:, cols], bricks.at[:, cols], sem.at[2 + k])
        copy.start()
        copies.append(copy)
    for c in copies:
        c.wait()


def vmem(*shape):
    return pltpu.VMEM(shape, F32)


def out(*shape, dtype=F32):
    return jax.ShapeDtypeStruct(shape, dtype)


def send(x, ds, dd, wrap_s, wrap_d):
    ns, nd = lax.axis_size("surf"), lax.axis_size("depth")
    pairs = [
        (s * nd + d, (s + ds) % ns * nd + (d + dd) % nd)
        for s in range(ns)
        for d in range(nd)
        if (wrap_s or 0 <= s + ds < ns) and (wrap_d or 0 <= d + dd < nd)
    ]
    return lax.ppermute(x, ("surf", "depth"), pairs)


def call(kernel, name, ins, outs, scratch=(), specs=None, out_space=pltpu.VMEM):
    here = pl.BlockSpec(memory_space=pltpu.VMEM)
    return pl.pallas_call(
        kernel,
        out_shape=tuple(outs),
        in_specs=specs or [here] * len(ins),
        out_specs=tuple(pl.BlockSpec(memory_space=out_space) for _ in outs),
        scratch_shapes=list(scratch),
        compiler_params=pltpu.CompilerParams(vmem_limit_bytes=48 * 1024 * 1024),
        name=name,
    )(*ins)


def in_hbm(x):
    return pltpu.with_memory_space_constraint(x, pltpu.HBM)


def per_device(
    wave_now, wave_old, adj_now, adj_old, source, adj_source,
    inv_density, inv_modulus, element_cell, send_elem, send_brick, send_count,
):
    shape = wave_now.shape
    wave, wave_old, adj, adj_old, source, adj_source = (
        x.reshape(4 * PLANE, 128)
        for x in (wave_now, wave_old, adj_now, adj_old, source, adj_source)
    )
    there = pl.BlockSpec(memory_space=pltpu.HBM)
    line, plane = call(
        pack_kernel, "pack", [in_hbm(x) for x in (wave_now, adj_now)], (out(8, 8, 128), out(8, 16, 128)),
        [pltpu.SemaphoreType.DMA((4,))], [there] * 2,
    )
    hc = send(line, 0, -1, True, True)
    prep = call(
        prep_kernel,
        "prep",
        [in_hbm(x) for x in (inv_density, inv_modulus, element_cell, send_elem, send_brick)]
        + [send_count],
        (out(128, 256), out(160, 128), out(8, 256), out(512, 640, dtype=BF16),
         out(640, 512, dtype=BF16), out(128, 128)),
        [vmem(125, 256), vmem(125, 256), pltpu.VMEM((1, 256), jnp.int32),
         pltpu.VMEM((1, 4, 256), jnp.int32), pltpu.VMEM((1, 4, 256), jnp.int32),
         pltpu.SemaphoreType.DMA((5,)), vmem(128, 128), vmem(128, 128), vmem(25, 512)],
        [there] * 5 + [pl.BlockSpec(memory_space=pltpu.SMEM)],
    )
    hc, plane, prep = lax.optimization_barrier((hc, plane, tuple(prep)))
    stiff, mass, targ, spread, fold, wcol = prep
    ha = send(jnp.concatenate([plane.reshape(128, 128), hc[:, 0]], 0), -1, 0, True, True)

    kern_low, ng_low, val_up, prod_up, frc_up = call(
        early_kernel,
        "early",
        (wave, adj, hc, stiff, spread, fold, wcol),
        (out(128, 128), out(8 * NROW, 128), out(160, 640), out(800, 128), out(160, 640)),
        [vmem(8 * NROW, 128), vmem(200, 512), vmem(200, 640), vmem(1000, 128), vmem(200, 640)],
    )
    ng, own, buf_s, buf_d, buf_sd = call(
        late_kernel,
        "late",
        (ha, stiff, spread, fold, wcol, kern_low, ng_low, mass, targ, val_up, prod_up, frc_up),
        (out(8 * NROW, 128), out(256, 128), out(400, 128), out(328, 128), out(272, 128)),
        [vmem(128, 128), vmem(8 * 17, 128), vmem(200, 512), vmem(40, 640),
         vmem(1000, 128), vmem(200, 640)],
    )
    got_s = send(buf_s, 1, 0, True, True)
    got_d = send(buf_d, 0, 1, True, True)
    got_sd = send(buf_sd, 1, 1, False, False)
    near, inner = call(
        near_kernel, "near", (own, got_d, ng_low, ng, mass), (out(128, 1024), out(9, 8, 16, 128))
    )
    wave_next, adj_next, bricks = call(
        final_kernel,
        "final",
        (wave, wave_old, adj, adj_old, source, adj_source, inner, near, got_s, got_d, got_sd),
        (out(4 * PLANE, 128), out(4 * PLANE, 128), out(125, 1024)),
        [vmem(4 * PLANE, 128), vmem(4 * PLANE, 128), vmem(125, 1024), pltpu.SemaphoreType.DMA((2 + CHUNKS,))],
        out_space=pl.ANY,
    )
    return wave_next.reshape(shape), adj_next.reshape(shape), bricks


def solution(mesh):
    field = P(None, "surf", "depth", None)
    both = ("surf", "depth")
    return jax.shard_map(
        per_device,
        mesh=mesh,
        in_specs=(field,) * 6
        + (P(None, both), P(None, both), P(both, None), P(both, None, None), P(both, None, None), P(both, None)),
        out_specs=(field, field, P(None, both)),
        check_vma=False,
    )
```

```python
import math

import jax
import jax.numpy as jnp
import numpy as np
from jax import lax
from jax.experimental import pallas as pl
from jax.experimental.pallas import tpu as pltpu
from jax.sharding import PartitionSpec as P

F32 = jnp.float32
BF16 = jnp.bfloat16
DT = 0.05
NT = (((1,), (1,)), ((), ()))
CHUNKS = 2
NROW = 85
COLUMN = 136
PLANE = 128


def gll():
    x = np.array([-1.0, -math.sqrt(3.0 / 7.0), 0.0, math.sqrt(3.0 / 7.0), 1.0])
    w = np.array([0.1, 49.0 / 90.0, 32.0 / 45.0, 49.0 / 90.0, 0.1])
    eye = np.eye(5)
    diff = x[:, None] - x[None, :] + eye
    prod = np.prod(diff, axis=1)
    deriv = prod[:, None] / prod[None, :] / diff
    inv = np.where(eye > 0.5, 0.0, 1.0 / diff)
    deriv = np.where(eye > 0.5, inv.sum(axis=1)[:, None], deriv)
    return deriv, w


DERIV, WEIGHT = gll()


def apply_deriv(mat, v):
    e0, e1, e2 = v[0] + v[4], v[1] + v[3], v[2]
    o0, o1 = v[0] - v[4], v[1] - v[3]
    half = lambda i, l: float(0.5 * (mat[i, l] + mat[i, 4 - l]))
    dif = lambda i, l: float(0.5 * (mat[i, l] - mat[i, 4 - l]))
    odd = [half(i, 0) * e0 + half(i, 1) * e1 + float(mat[i, 2]) * e2 for i in (0, 1)]
    even = [dif(i, 0) * o0 + dif(i, 1) * o1 for i in (0, 1, 2)]
    return [even[0] + odd[0], even[1] + odd[1], even[2], even[1] - odd[1], even[0] - odd[0]]


def split2(x):
    hi = x.astype(BF16)
    return hi, (x - hi.astype(F32)).astype(BF16)


def dot2(x, table, dims=(((1,), (0,)), ((), ()))):
    hi, lo = split2(x)
    rows = x.shape[0]
    if rows % 16 == 0:
        both = jnp.concatenate([hi, lo], axis=0)
        both = lax.dot_general(both, table, dims, preferred_element_type=F32)
        return both[0:rows] + both[rows:]
    return lax.dot_general(hi, table, dims, preferred_element_type=F32) + lax.dot_general(
        lo, table, dims, preferred_element_type=F32
    )


def pack_kernel(wave, adj, line, plane, sem):
    copies = []
    for k, src in enumerate((wave, adj)):
        to = pl.ds(4 * k, 4)
        copies.append(pltpu.make_async_copy(src.at[:, :, 0, :], line.at[to], sem.at[2 * k]))
        copies.append(pltpu.make_async_copy(src.at[:, 0], plane.at[to], sem.at[2 * k + 1]))
    for c in copies:
        c.start()
    for c in copies:
        c.wait()


def prep_kernel(
    wave_hbm, adj_hbm, dens_hbm, modu_hbm, cell_hbm, selem_hbm, sbrick_hbm, scount_hbm,
    fields, stiff, mass, targ, spread, fold, wcol,
    dens, modu, cell, selem, sbrick, scount, sem, ms0, ms1, mo,
):
    pairs = (
        (dens_hbm, dens), (modu_hbm, modu), (cell_hbm, cell), (selem_hbm, selem), (sbrick_hbm, sbrick),
        (scount_hbm, scount),
    )
    copies = [pltpu.make_async_copy(a, b, sem.at[k]) for k, (a, b) in enumerate(pairs)]
    late_copies = []
    for x in range(8):
        src = (wave_hbm if x < 4 else adj_hbm).at[pl.ds(x % 4 * PLANE, PLANE)]
        late_copies.append(pltpu.make_async_copy(src, fields.at[pl.ds(x * COLUMN, PLANE)], sem.at[6 + x]))
    for c in copies + late_copies:
        c.start()
    sub = lax.broadcasted_iota(jnp.int32, (128, 128), 0)
    lane = lax.broadcasted_iota(jnp.int32, (128, 128), 1)
    fold[...] = jnp.zeros(fold.shape, BF16)
    for r in range(4):
        node = (4 * (lane & 31) + r) & 127
        hit = sub == node
        for ec in range(4):
            spread[ec * 128 : ec * 128 + 128, r * 128 : r * 128 + 128] = jnp.where(
                hit & ((lane >> 5) == ec), 1.0, 0.0
            ).astype(BF16)
        back = jnp.where(lane == ((4 * (sub & 31) + r) & 127), 1.0, 0.0).astype(BF16)
        for ec in range(4):
            rows = slice(r * 128 + ec * 32, r * 128 + ec * 32 + 32)
            fold[rows, ec * 128 : ec * 128 + 128] = back[ec * 32 : ec * 32 + 32]

    def weight(i):
        edge = float(WEIGHT[0])
        return jnp.where(
            i == 2, float(WEIGHT[2]), jnp.where((i == 0) | (i == 4), edge, float(WEIGHT[1]))
        )

    p = (sub >= 25).astype(jnp.int32) + (sub >= 50) + (sub >= 75) + (sub >= 100) + (sub >= 125)
    rest = sub - 25 * p
    q = (rest >= 5).astype(jnp.int32) + (rest >= 10) + (rest >= 15) + (rest >= 20)
    cub = weight(p) * weight(q) * weight(rest - 5 * q)
    wcol[...] = cub * -DT
    for c in copies:
        c.wait()
    both = jnp.concatenate([cub[0:125], cub[0:125]], axis=1)
    place = (lax.broadcasted_iota(jnp.int32, (256, 256), 0) == cell[...]).astype(F32).astype(BF16)
    stiff[0:125, :] = dot2(dens[...], place, NT) * both
    cells = dot2(modu[...], place, NT) * both
    mass[...] = jnp.zeros(mass.shape, F32)
    lined = []
    for ea, ms in ((0, ms0), (1, ms1)):
        ms[0:125, :] = cells[:, ea * 128 : ea * 128 + 128]
        ms[125:160, :] = jnp.zeros((35, 128), F32)
        parts = [ms[pl.ds(r, 32, stride=5), :] for r in range(5)]
        parts[0] = parts[0] + to_next(parts.pop())
        lined.append(jnp.concatenate(parts, axis=1))
    mo[...] = dot2(jnp.concatenate(lined, axis=0), fold[...])
    for ea in range(2):
        for p in range(5):
            for ec in range(4):
                at = pl.ds((4 * ea + p) * 17 + 4 * ec, 5)
                row = ea * 32 + p * 5
                mass[at, :] = mass[at, :] + mo[row : row + 5, ec * 128 : ec * 128 + 128]
    sub = lax.broadcasted_iota(jnp.int32, (8, 256), 0)
    lane = lax.broadcasted_iota(jnp.int32, (1, 256), 1)
    elem_iota = lax.broadcasted_iota(jnp.int32, (256, 256), 0)
    acc = jnp.zeros((8, 256), F32)
    for t in range(4):
        brick = jnp.where(lane < scount[0, t], sbrick[0, t : t + 1, :] + 1, 0)
        high = lax.shift_right_logical(brick, 5)
        low = brick - high * 32
        rows = jnp.where(sub == t, high, jnp.where(sub == t + 4, low, 0))
        pick = (elem_iota == selem[0, t : t + 1, :]).astype(F32).astype(BF16)
        acc = acc + lax.dot_general(
            rows.astype(F32).astype(BF16), pick, NT, preferred_element_type=F32
        )
    at_cell = lax.dot_general(acc.astype(BF16), place, NT, preferred_element_type=F32)
    targ[0:4, :] = 32.0 * at_cell[0:4] + at_cell[4:8] - 1.0
    for c in late_copies:
        c.wait()


def load_plane(row_of, lhs, row):
    for c in range(17):
        tile = row_of(c)
        if c < 16:
            at = row + c % 4 * 8
            lhs[at : at + 8, c // 4 * 128 : c // 4 * 128 + 128] = tile
        if c % 4 == 0 and c > 0:
            lhs[row + 32 : row + 40, (c // 4 - 1) * 128 : c // 4 * 128] = tile


def from_next(x):
    last = (lax.broadcasted_iota(jnp.int32, x.shape, 1) & 31) == 31
    return jnp.where(last, pltpu.roll(x, 31, 1), pltpu.roll(x, 127, 1))


def to_next(x):
    zeroth = (lax.broadcasted_iota(jnp.int32, x.shape, 1) & 31) == 0
    return jnp.where(zeroth, pltpu.roll(x, 97, 1), pltpu.roll(x, 1, 1))


def spread_planes(val, row, planes, spread):
    nodes = dot2(planes, spread[...])
    val[row : row + planes.shape[0], 0:512] = nodes
    val[row : row + planes.shape[0], 512:640] = from_next(nodes[:, 0:128])


def node_tile(p, q, r):
    return (slice((p * 5 + q) * 8, (p * 5 + q) * 8 + 8), slice(r * 128, r * 128 + 128))


def node_rows(p, q, r):
    at = (p * 25 + q * 5 + r) * 8
    return slice(at, at + 8)


def line_terms(ea, nodes, values, stiff):
    lanes = slice(ea * 128, ea * 128 + 128)
    grad = apply_deriv(DERIV, values)
    flux = []
    for k, (p, q, r) in enumerate(nodes):
        at = p * 25 + q * 5 + r
        flux.append(grad[k] * stiff[at : at + 1, lanes])
    return [g * pltpu.roll(g, 4, 0) for g in grad], apply_deriv(DERIV.T, flux)


def inside_plane(ea, p, val, at, stiff, prod, frc):
    for i in range(5):
        nodes = [(p, k, i) for k in range(5)]
        pair, force = line_terms(ea, nodes, [val[node_tile(at, k, i)] for k in range(5)], stiff)
        for k, n in enumerate(nodes):
            prod[node_rows(*n), :] = pair[k]
            frc[node_tile(*n)] = force[k]
    for i in range(5):
        nodes = [(p, i, k) for k in range(5)]
        pair, force = line_terms(ea, nodes, [val[node_tile(at, i, k)] for k in range(5)], stiff)
        for k, n in enumerate(nodes):
            prod[node_rows(*n), :] = prod[node_rows(*n), :] + pair[k]
            frc[node_tile(*n)] = frc[node_tile(*n)] + force[k]


def across_planes(ea, val, last, stiff, prod_in, frc_in, prod, frc):
    for q in range(5):
        for r in range(5):
            nodes = [(k, q, r) for k in range(5)]
            values = [val[node_tile(k, q, r)] for k in range(4)] + [last(q, r)]
            pair, force = line_terms(ea, nodes, values, stiff)
            for k, n in enumerate(nodes):
                old_p, old_f = (prod_in, frc_in) if k < 4 else (prod, frc)
                prod[node_rows(*n), :] = old_p[node_rows(*n), :] + pair[k]
                frc[node_tile(*n)] = old_f[node_tile(*n)] + force[k]


def finish_layer(prod, frc, lhs, fold, wcol, kern, ng):
    for j in range(16):
        count = 8 if j < 15 else 5
        total = sum(prod[pl.ds(j * 64 + t, count, stride=8), :] for t in range(4))
        kern[j * 8 : j * 8 + count, :] = total * wcol[j * 8 : j * 8 + count, :]
    kern[125:128, :] = jnp.zeros((3, 128), F32)
    zeroth = frc[:, 0:128] + to_next(frc[:, 512:640])
    lhs[...] = dot2(jnp.concatenate([zeroth, frc[:, 128:512]], axis=1), fold[...])
    for p in range(5):
        for c in range(17):
            parts = []
            if c < 16:
                at = (p * 5 + c % 4) * 8
                parts.append(lhs[at : at + 8, c // 4 * 128 : c // 4 * 128 + 128])
            if c % 4 == 0 and c > 0:
                at = (p * 5 + 4) * 8
                parts.append(lhs[at : at + 8, (c // 4 - 1) * 128 : c // 4 * 128])
            ng[pl.ds(p * 17 + c, 8, stride=NROW), :] = sum(parts)


def early_kernel(
    fields, hc, stiff, spread, fold, wcol, kern, ng, val_up, prod_up, frc_up, lhs, val, prod, frc
):
    keep = (lax.axis_index("depth") < lax.axis_size("depth") - 1).astype(F32)

    def field_row(a):
        def row_of(c):
            if c == 16:
                return hc[pl.ds(a, 8, stride=8), :] * keep
            return fields[pl.ds(a * 16 + c, 8, stride=COLUMN), :]

        return row_of

    for a in range(5):
        load_plane(field_row(a), lhs, a * 40)
    spread_planes(val, 0, lhs[...], spread)
    for p in range(5):
        inside_plane(0, p, val, p, stiff, prod, frc)
    across_planes(0, val, lambda q, r: val[node_tile(4, q, r)], stiff, prod, frc, prod, frc)
    finish_layer(prod, frc, lhs, fold, wcol, kern, ng)
    val_up[0:40, :] = val[160:200, :]
    for a in range(5, 8):
        load_plane(field_row(a), lhs, (a - 5) * 40)
    spread_planes(val_up, 40, lhs[0:120, :], spread)
    for p in range(4):
        inside_plane(1, p, val_up, p, stiff, prod_up, frc_up)


def late_kernel(
    ha, stiff, spread, fold, wcol, kern_low, ng_low, mass, targ, val_up, prod_up, frc_up,
    ng, own, buf_s, buf_d, buf_sd, kern, lhs, val, prod, frc,
):
    keep_d = (lax.axis_index("depth") < lax.axis_size("depth") - 1).astype(F32)
    keep_s = (lax.axis_index("surf") < lax.axis_size("surf") - 1).astype(F32)

    def row_of(c):
        if c == 16:
            return ha[128:136, :] * (keep_s * keep_d)
        return ha[pl.ds(c, 8, stride=16), :] * keep_s

    load_plane(row_of, lhs, 0)
    spread_planes(val, 0, lhs[0:40, :], spread)
    inside_plane(1, 4, val, 0, stiff, prod, frc)
    across_planes(1, val_up, lambda q, r: val[node_tile(0, q, r)], stiff, prod_up, frc_up, prod, frc)
    finish_layer(prod, frc, lhs, fold, wcol, kern, ng)
    for row, buf in ((0, own), (1, buf_s), (2, buf_d), (3, buf_sd)):
        buf[0:128, :] = kern_low[...]
        buf[128:256, :] = kern[...]
        buf[125:126, :] = targ[row : row + 1, 0:128]
        buf[253:254, :] = targ[row : row + 1, 128:256]
    for x in range(8):
        base = x * NROW
        for a in range(8):
            at = base + a * 17 + 16
            if a < 4:
                row = ng_low[at : at + 1, :]
            elif a == 4:
                row = ng_low[at : at + 1, :] + ng[base + 16 : base + 17, :]
            else:
                row = ng[at - 68 : at - 67, :]
            buf_d[256 + x * 8 + a : 257 + x * 8 + a, :] = row
        buf_s[256 + x * 16 : 272 + x * 16, :] = ng[base + 68 : base + 84, :]
        buf_sd[256 + x : 257 + x, :] = ng[base + 84 : base + 85, :]
    for a in range(8):
        buf_d[320 + a : 321 + a, :] = mass[a * 17 + 16 : a * 17 + 17, :]
    buf_s[384:400, :] = mass[136:152, :]
    buf_sd[264:265, :] = mass[152:153, :]
    buf_sd[265:272, :] = jnp.zeros((7, 128), F32)


def add_bricks(acc, buf, first=0, count=1024):
    bricks = lax.broadcasted_iota(jnp.int32, (count, 128), 0).astype(F32) + float(first)
    for ea in range(2):
        block = buf[ea * 128 : ea * 128 + 128, :]
        hit = jnp.where(bricks == block[125:126, :], 1.0, 0.0).astype(BF16)
        term = dot2(block, hit, NT)
        acc = term if acc is None else acc + term
    return acc


def near_kernel(own, got_d, ng_low, ng, mass, near, inner):
    near[...] = add_bricks(add_bricks(None, own), got_d)
    for x in range(8):
        for a in range(8):
            low, high = x * NROW + a * 17, x * NROW + (a - 4) * 17
            if a < 4:
                inner[x, a] = ng_low[low : low + 16, :]
            elif a == 4:
                inner[x, a] = ng_low[low : low + 16, :] + ng[high : high + 16, :]
            else:
                inner[x, a] = ng[high : high + 16, :]
    for a in range(8):
        inner[8, a] = mass[a * 17 : a * 17 + 16, :]


def final_kernel(
    fields, wave_old, adj_old, src, adj_src, inner, near, got_s, got_d, got_sd,
    wave_next, adj_next, bricks, wave_buf, adj_buf, brick_buf, sem,
):
    keep_s = (lax.axis_index("surf") > 0).astype(F32)
    keep_d = (lax.axis_index("depth") > 0).astype(F32)
    first = lax.broadcasted_iota(jnp.int32, (16, 128), 0) == 0

    def total(ch, a):
        part = inner[ch, a]
        line = got_d[256 + ch * 8 + a : 257 + ch * 8 + a, :] * keep_d
        if a == 0:
            part = part + got_s[256 + ch * 16 : 272 + ch * 16, :] * keep_s
            line = line + got_sd[256 + ch : 257 + ch, :] * (keep_s * keep_d)
        return part + jnp.where(first, line, 0.0)

    for a in range(8):
        scale = (DT * DT) / total(8, a)
        for t in range(4):
            at = slice(t * PLANE + a * 16, t * PLANE + a * 16 + 16)
            now = slice(t * COLUMN + a * 16, t * COLUMN + a * 16 + 16)
            adj = slice(now.start + 4 * COLUMN, now.stop + 4 * COLUMN)
            wave_buf[at, :] = 2.0 * fields[now, :] - wave_old[at, :] + (src[at, :] - total(t, a)) * scale
            adj_buf[at, :] = (
                2.0 * fields[adj, :] - adj_old[at, :] + (adj_src[at, :] - total(4 + t, a)) * scale
            )
    copies = [
        pltpu.make_async_copy(wave_buf, wave_next, sem.at[0]),
        pltpu.make_async_copy(adj_buf, adj_next, sem.at[1]),
    ]
    for c in copies:
        c.start()
    for k in range(CHUNKS):
        cols = slice(k * (1024 // CHUNKS), (k + 1) * (1024 // CHUNKS))
        acc = near[:, cols]
        for buf in (got_s, got_sd):
            acc = add_bricks(acc, buf, k * (1024 // CHUNKS), 1024 // CHUNKS)
        brick_buf[:, cols] = acc[0:125, :]
        copy = pltpu.make_async_copy(brick_buf.at[:, cols], bricks.at[:, cols], sem.at[2 + k])
        copy.start()
        copies.append(copy)
    for c in copies:
        c.wait()


def vmem(*shape):
    return pltpu.VMEM(shape, F32)


def out(*shape, dtype=F32):
    return jax.ShapeDtypeStruct(shape, dtype)


def send(x, ds, dd, wrap_s, wrap_d):
    ns, nd = lax.axis_size("surf"), lax.axis_size("depth")
    pairs = [
        (s * nd + d, (s + ds) % ns * nd + (d + dd) % nd)
        for s in range(ns)
        for d in range(nd)
        if (wrap_s or 0 <= s + ds < ns) and (wrap_d or 0 <= d + dd < nd)
    ]
    return lax.ppermute(x, ("surf", "depth"), pairs)


def call(kernel, name, ins, outs, scratch=(), specs=None, out_space=pltpu.VMEM):
    here = pl.BlockSpec(memory_space=pltpu.VMEM)
    return pl.pallas_call(
        kernel,
        out_shape=tuple(outs),
        in_specs=specs or [here] * len(ins),
        out_specs=tuple(pl.BlockSpec(memory_space=out_space) for _ in outs),
        scratch_shapes=list(scratch),
        compiler_params=pltpu.CompilerParams(vmem_limit_bytes=48 * 1024 * 1024),
        name=name,
    )(*ins)


def in_hbm(x):
    return pltpu.with_memory_space_constraint(x, pltpu.HBM)


def per_device(
    wave_now, wave_old, adj_now, adj_old, source, adj_source,
    inv_density, inv_modulus, element_cell, send_elem, send_brick, send_count,
):
    shape = wave_now.shape
    wave, wave_old, adj, adj_old, source, adj_source = (
        x.reshape(4 * PLANE, 128)
        for x in (wave_now, wave_old, adj_now, adj_old, source, adj_source)
    )
    there = pl.BlockSpec(memory_space=pltpu.HBM)
    line, plane = call(
        pack_kernel, "pack", [in_hbm(x) for x in (wave_now, adj_now)], (out(8, 8, 128), out(8, 16, 128)),
        [pltpu.SemaphoreType.DMA((4,))], [there] * 2,
    )
    hc = send(line, 0, -1, True, True)
    prep = call(
        prep_kernel,
        "prep",
        [in_hbm(x) for x in (wave, adj, inv_density, inv_modulus, element_cell, send_elem, send_brick, send_count)],
        (out(8 * COLUMN, 128), out(128, 256), out(160, 128), out(8, 256),
         out(512, 512, dtype=BF16), out(512, 512, dtype=BF16), out(128, 128)),
        [vmem(125, 256), vmem(125, 256), pltpu.VMEM((1, 256), jnp.int32),
         pltpu.VMEM((1, 4, 256), jnp.int32), pltpu.VMEM((1, 4, 256), jnp.int32),
         pltpu.SMEM((1, 4), jnp.int32), pltpu.SemaphoreType.DMA((14,)), vmem(160, 128), vmem(160, 128), vmem(64, 512)],
        [there] * 8,
    )
    hc, plane, prep = lax.optimization_barrier((hc, plane, tuple(prep)))
    fields, stiff, mass, targ, spread, fold, wcol = prep
    ha = send(jnp.concatenate([plane.reshape(128, 128), hc[:, 0]], 0), -1, 0, True, True)

    kern_low, ng_low, val_up, prod_up, frc_up = call(
        early_kernel,
        "early",
        (fields, hc.reshape(64, 128), stiff, spread, fold, wcol),
        (out(128, 128), out(8 * NROW, 128), out(160, 640), out(800, 128), out(160, 640)),
        [vmem(200, 512), vmem(200, 640), vmem(1000, 128), vmem(200, 640)],
    )
    ng, own, buf_s, buf_d, buf_sd = call(
        late_kernel,
        "late",
        (ha, stiff, spread, fold, wcol, kern_low, ng_low, mass, targ, val_up, prod_up, frc_up),
        (out(8 * NROW, 128), out(256, 128), out(400, 128), out(328, 128), out(272, 128)),
        [vmem(128, 128), vmem(200, 512), vmem(40, 640),
         vmem(1000, 128), vmem(200, 640)],
    )
    got_s = send(buf_s, 1, 0, True, True)
    got_d = send(buf_d, 0, 1, True, True)
    got_sd = send(buf_sd, 1, 1, False, False)
    near, inner = call(
        near_kernel, "near", (own, got_d, ng_low, ng, mass), (out(128, 1024), out(9, 8, 16, 128))
    )
    wave_next, adj_next, bricks = call(
        final_kernel,
        "final",
        (fields, wave_old, adj_old, source, adj_source, inner, near, got_s, got_d, got_sd),
        (out(4 * PLANE, 128), out(4 * PLANE, 128), out(125, 1024)),
        [vmem(4 * PLANE, 128), vmem(4 * PLANE, 128), vmem(125, 1024), pltpu.SemaphoreType.DMA((2 + CHUNKS,))],
        out_space=pl.ANY,
    )
    return wave_next.reshape(shape), adj_next.reshape(shape), bricks


def solution(mesh):
    field = P(None, "surf", "depth", None)
    both = ("surf", "depth")
    return jax.shard_map(
        per_device,
        mesh=mesh,
        in_specs=(field,) * 6
        + (P(None, both), P(None, both), P(both, None), P(both, None, None), P(both, None, None), P(both, None)),
        out_specs=(field, field, P(None, both)),
        check_vma=False,
    )
```

```python
import math

import jax
import jax.numpy as jnp
import numpy as np
from jax import lax
from jax.experimental import pallas as pl
from jax.experimental.pallas import tpu as pltpu
from jax.sharding import PartitionSpec as P

F32 = jnp.float32
BF16 = jnp.bfloat16
DT = 0.05
NT = (((1,), (1,)), ((), ()))
CHUNKS = 2
NROW = 85
COLUMN = 136
PLANE = 128


def gll():
    x = np.array([-1.0, -math.sqrt(3.0 / 7.0), 0.0, math.sqrt(3.0 / 7.0), 1.0])
    w = np.array([0.1, 49.0 / 90.0, 32.0 / 45.0, 49.0 / 90.0, 0.1])
    eye = np.eye(5)
    diff = x[:, None] - x[None, :] + eye
    prod = np.prod(diff, axis=1)
    deriv = prod[:, None] / prod[None, :] / diff
    inv = np.where(eye > 0.5, 0.0, 1.0 / diff)
    deriv = np.where(eye > 0.5, inv.sum(axis=1)[:, None], deriv)
    return deriv, w


DERIV, WEIGHT = gll()


def apply_deriv(mat, v):
    e0, e1, e2 = v[0] + v[4], v[1] + v[3], v[2]
    o0, o1 = v[0] - v[4], v[1] - v[3]
    half = lambda i, l: float(0.5 * (mat[i, l] + mat[i, 4 - l]))
    dif = lambda i, l: float(0.5 * (mat[i, l] - mat[i, 4 - l]))
    odd = [half(i, 0) * e0 + half(i, 1) * e1 + float(mat[i, 2]) * e2 for i in (0, 1)]
    even = [dif(i, 0) * o0 + dif(i, 1) * o1 for i in (0, 1, 2)]
    return [even[0] + odd[0], even[1] + odd[1], even[2], even[1] - odd[1], even[0] - odd[0]]


def split2(x):
    hi = x.astype(BF16)
    return hi, (x - hi.astype(F32)).astype(BF16)


def dot2(x, table, dims=(((1,), (0,)), ((), ()))):
    hi, lo = split2(x)
    rows = x.shape[0]
    if rows % 16 == 0:
        both = jnp.concatenate([hi, lo], axis=0)
        both = lax.dot_general(both, table, dims, preferred_element_type=F32)
        return both[0:rows] + both[rows:]
    return lax.dot_general(hi, table, dims, preferred_element_type=F32) + lax.dot_general(
        lo, table, dims, preferred_element_type=F32
    )


def pack_kernel(wave, adj, line, plane, sem):
    copies = []
    for k, src in enumerate((wave, adj)):
        to = pl.ds(4 * k, 4)
        copies.append(pltpu.make_async_copy(src.at[:, :, 0, :], line.at[to], sem.at[2 * k]))
        copies.append(pltpu.make_async_copy(src.at[:, 0], plane.at[to], sem.at[2 * k + 1]))
    for c in copies:
        c.start()
    for c in copies:
        c.wait()


def prep_kernel(
    wave_hbm, adj_hbm, dens_hbm, modu_hbm, cell_hbm, selem_hbm, sbrick_hbm, scount_hbm,
    fields, stiff, mass, targ, spread, fold, wcol,
    dens, modu, cell, selem, sbrick, scount, sem, ms0, ms1, mo,
):
    pairs = (
        (dens_hbm, dens), (modu_hbm, modu), (cell_hbm, cell), (selem_hbm, selem), (sbrick_hbm, sbrick),
        (scount_hbm, scount),
    )
    copies = [pltpu.make_async_copy(a, b, sem.at[k]) for k, (a, b) in enumerate(pairs)]
    late_copies = []
    for x in range(8):
        src = (wave_hbm if x < 4 else adj_hbm).at[pl.ds(x % 4 * PLANE, PLANE)]
        late_copies.append(pltpu.make_async_copy(src, fields.at[pl.ds(x * COLUMN, PLANE)], sem.at[6 + x]))
    for c in copies + late_copies:
        c.start()
    sub = lax.broadcasted_iota(jnp.int32, (128, 128), 0)
    lane = lax.broadcasted_iota(jnp.int32, (128, 128), 1)
    fold[...] = jnp.zeros(fold.shape, BF16)
    for r in range(4):
        node = (4 * (lane & 31) + r) & 127
        hit = sub == node
        for ec in range(4):
            spread[ec * 128 : ec * 128 + 128, r * 128 : r * 128 + 128] = jnp.where(
                hit & ((lane >> 5) == ec), 1.0, 0.0
            ).astype(BF16)
        back = jnp.where(lane == ((4 * (sub & 31) + r) & 127), 1.0, 0.0).astype(BF16)
        for ec in range(4):
            rows = slice(r * 128 + ec * 32, r * 128 + ec * 32 + 32)
            fold[rows, ec * 128 : ec * 128 + 128] = back[ec * 32 : ec * 32 + 32]

    def weight(i):
        edge = float(WEIGHT[0])
        return jnp.where(
            i == 2, float(WEIGHT[2]), jnp.where((i == 0) | (i == 4), edge, float(WEIGHT[1]))
        )

    p = (sub >= 25).astype(jnp.int32) + (sub >= 50) + (sub >= 75) + (sub >= 100) + (sub >= 125)
    rest = sub - 25 * p
    q = (rest >= 5).astype(jnp.int32) + (rest >= 10) + (rest >= 15) + (rest >= 20)
    cub = weight(p) * weight(q) * weight(rest - 5 * q)
    wcol[...] = cub * -DT
    for c in copies:
        c.wait()
    both = jnp.concatenate([cub[0:125], cub[0:125]], axis=1)
    place = (lax.broadcasted_iota(jnp.int32, (256, 256), 0) == cell[...]).astype(F32).astype(BF16)
    stiff[0:125, :] = dot2(dens[...], place, NT) * both
    cells = dot2(modu[...], place, NT) * both
    mass[...] = jnp.zeros(mass.shape, F32)
    lined = []
    for ea, ms in ((0, ms0), (1, ms1)):
        ms[0:125, :] = cells[:, ea * 128 : ea * 128 + 128]
        ms[125:160, :] = jnp.zeros((35, 128), F32)
        parts = [ms[pl.ds(r, 32, stride=5), :] for r in range(5)]
        parts[0] = parts[0] + to_next(parts.pop())
        lined.append(jnp.concatenate(parts, axis=1))
    mo[...] = dot2(jnp.concatenate(lined, axis=0), fold[...])
    for ea in range(2):
        for p in range(5):
            for ec in range(4):
                at = pl.ds((4 * ea + p) * 17 + 4 * ec, 5)
                row = ea * 32 + p * 5
                mass[at, :] = mass[at, :] + mo[row : row + 5, ec * 128 : ec * 128 + 128]
    sub = lax.broadcasted_iota(jnp.int32, (8, 256), 0)
    lane = lax.broadcasted_iota(jnp.int32, (1, 256), 1)
    elem_iota = lax.broadcasted_iota(jnp.int32, (256, 256), 0)
    acc = jnp.zeros((8, 256), F32)
    for t in range(4):
        brick = jnp.where(lane < scount[0, t], sbrick[0, t : t + 1, :] + 1, 0)
        high = lax.shift_right_logical(brick, 5)
        low = brick - high * 32
        rows = jnp.where(sub == t, high, jnp.where(sub == t + 4, low, 0))
        pick = (elem_iota == selem[0, t : t + 1, :]).astype(F32).astype(BF16)
        acc = acc + lax.dot_general(
            rows.astype(F32).astype(BF16), pick, NT, preferred_element_type=F32
        )
    at_cell = lax.dot_general(acc.astype(BF16), place, NT, preferred_element_type=F32)
    targ[0:4, :] = 32.0 * at_cell[0:4] + at_cell[4:8] - 1.0
    for c in late_copies:
        c.wait()


def load_plane(row_of, lhs, row):
    for c in range(17):
        tile = row_of(c)
        if c < 16:
            at = row + c % 4 * 8
            lhs[at : at + 8, c // 4 * 128 : c // 4 * 128 + 128] = tile
        if c % 4 == 0 and c > 0:
            lhs[row + 32 : row + 40, (c // 4 - 1) * 128 : c // 4 * 128] = tile


def from_next(x):
    last = (lax.broadcasted_iota(jnp.int32, x.shape, 1) & 31) == 31
    return jnp.where(last, pltpu.roll(x, 31, 1), pltpu.roll(x, 127, 1))


def to_next(x):
    zeroth = (lax.broadcasted_iota(jnp.int32, x.shape, 1) & 31) == 0
    return jnp.where(zeroth, pltpu.roll(x, 97, 1), pltpu.roll(x, 1, 1))


def spread_planes(val, row, planes, spread):
    nodes = dot2(planes, spread[...])
    val[row : row + planes.shape[0], 0:512] = nodes
    val[row : row + planes.shape[0], 512:640] = from_next(nodes[:, 0:128])


def node_tile(p, q, r):
    return (slice((p * 5 + q) * 8, (p * 5 + q) * 8 + 8), slice(r * 128, r * 128 + 128))


def node_rows(p, q, r):
    at = (p * 25 + q * 5 + r) * 8
    return slice(at, at + 8)


def line_terms(ea, nodes, values, stiff):
    lanes = slice(ea * 128, ea * 128 + 128)
    grad = apply_deriv(DERIV, values)
    flux = []
    for k, (p, q, r) in enumerate(nodes):
        at = p * 25 + q * 5 + r
        flux.append(grad[k] * stiff[at : at + 1, lanes])
    return [g * pltpu.roll(g, 4, 0) for g in grad], apply_deriv(DERIV.T, flux)


def inside_plane(ea, p, val, at, stiff, prod, frc):
    for i in range(5):
        nodes = [(p, k, i) for k in range(5)]
        pair, force = line_terms(ea, nodes, [val[node_tile(at, k, i)] for k in range(5)], stiff)
        for k, n in enumerate(nodes):
            prod[node_rows(*n), :] = pair[k]
            frc[node_tile(*n)] = force[k]
    for i in range(5):
        nodes = [(p, i, k) for k in range(5)]
        pair, force = line_terms(ea, nodes, [val[node_tile(at, i, k)] for k in range(5)], stiff)
        for k, n in enumerate(nodes):
            prod[node_rows(*n), :] = prod[node_rows(*n), :] + pair[k]
            frc[node_tile(*n)] = frc[node_tile(*n)] + force[k]


def across_planes(ea, val, last, stiff, prod_in, frc_in, prod, frc):
    for q in range(5):
        for r in range(5):
            nodes = [(k, q, r) for k in range(5)]
            values = [val[node_tile(k, q, r)] for k in range(4)] + [last(q, r)]
            pair, force = line_terms(ea, nodes, values, stiff)
            for k, n in enumerate(nodes):
                old_p, old_f = (prod_in, frc_in) if k < 4 else (prod, frc)
                prod[node_rows(*n), :] = old_p[node_rows(*n), :] + pair[k]
                frc[node_tile(*n)] = old_f[node_tile(*n)] + force[k]


def finish_layer(prod, frc, lhs, fold, wcol, kern, ng):
    for j in range(16):
        count = 8 if j < 15 else 5
        total = sum(prod[pl.ds(j * 64 + t, count, stride=8), :] for t in range(4))
        kern[j * 8 : j * 8 + count, :] = total * wcol[j * 8 : j * 8 + count, :]
    kern[125:128, :] = jnp.zeros((3, 128), F32)
    zeroth = frc[:, 0:128] + to_next(frc[:, 512:640])
    lhs[...] = dot2(jnp.concatenate([zeroth, frc[:, 128:512]], axis=1), fold[...])
    for p in range(5):
        for c in range(17):
            parts = []
            if c < 16:
                at = (p * 5 + c % 4) * 8
                parts.append(lhs[at : at + 8, c // 4 * 128 : c // 4 * 128 + 128])
            if c % 4 == 0 and c > 0:
                at = (p * 5 + 4) * 8
                parts.append(lhs[at : at + 8, (c // 4 - 1) * 128 : c // 4 * 128])
            ng[pl.ds(p * 17 + c, 8, stride=NROW), :] = sum(parts)


def early_kernel(
    fields, hc, stiff, spread, fold, wcol, kern, ng, val_up, prod_up, frc_up, lhs, val, prod, frc
):
    keep = (lax.axis_index("depth") < lax.axis_size("depth") - 1).astype(F32)

    def field_row(a):
        def row_of(c):
            if c == 16:
                return hc[pl.ds(a, 8, stride=8), :] * keep
            return fields[pl.ds(a * 16 + c, 8, stride=COLUMN), :]

        return row_of

    for a in range(5):
        load_plane(field_row(a), lhs, a * 40)
    spread_planes(val, 0, lhs[...], spread)
    for p in range(5):
        inside_plane(0, p, val, p, stiff, prod, frc)
    across_planes(0, val, lambda q, r: val[node_tile(4, q, r)], stiff, prod, frc, prod, frc)
    finish_layer(prod, frc, lhs, fold, wcol, kern, ng)
    val_up[0:40, :] = val[160:200, :]
    for a in range(5, 8):
        load_plane(field_row(a), lhs, (a - 5) * 40)
    spread_planes(val_up, 40, lhs[0:120, :], spread)
    for p in range(4):
        inside_plane(1, p, val_up, p, stiff, prod_up, frc_up)


def late_kernel(
    ha, stiff, spread, fold, wcol, kern_low, ng_low, mass, targ, val_up, prod_up, frc_up,
    ng, own, buf_s, buf_d, buf_sd, kern, lhs, val, prod, frc,
):
    keep_d = (lax.axis_index("depth") < lax.axis_size("depth") - 1).astype(F32)
    keep_s = (lax.axis_index("surf") < lax.axis_size("surf") - 1).astype(F32)

    def row_of(c):
        if c == 16:
            return ha[128:136, :] * (keep_s * keep_d)
        return ha[pl.ds(c, 8, stride=16), :] * keep_s

    load_plane(row_of, lhs, 0)
    spread_planes(val, 0, lhs[0:40, :], spread)
    inside_plane(1, 4, val, 0, stiff, prod, frc)
    across_planes(1, val_up, lambda q, r: val[node_tile(0, q, r)], stiff, prod_up, frc_up, prod, frc)
    finish_layer(prod, frc, lhs, fold, wcol, kern, ng)
    for row, buf in ((0, own), (1, buf_s), (2, buf_d), (3, buf_sd)):
        buf[0:128, :] = kern_low[...]
        buf[128:256, :] = kern[...]
        buf[125:126, :] = targ[row : row + 1, 0:128]
        buf[253:254, :] = targ[row : row + 1, 128:256]
    for x in range(8):
        base = x * NROW
        for a in range(8):
            at = base + a * 17 + 16
            if a < 4:
                row = ng_low[at : at + 1, :]
            elif a == 4:
                row = ng_low[at : at + 1, :] + ng[base + 16 : base + 17, :]
            else:
                row = ng[at - 68 : at - 67, :]
            buf_d[256 + x * 8 + a : 257 + x * 8 + a, :] = row
        buf_s[256 + x * 16 : 272 + x * 16, :] = ng[base + 68 : base + 84, :]
        buf_sd[256 + x : 257 + x, :] = ng[base + 84 : base + 85, :]
    for a in range(8):
        buf_d[320 + a : 321 + a, :] = mass[a * 17 + 16 : a * 17 + 17, :]
    buf_s[384:400, :] = mass[136:152, :]
    buf_sd[264:265, :] = mass[152:153, :]
    buf_sd[265:272, :] = jnp.zeros((7, 128), F32)


def brick_sums(bufs, first=0, count=1024):
    blocks = jnp.concatenate([buf[at : at + 128, :] for buf in bufs for at in (0, 128)], axis=1)
    target = blocks[125:126, :]
    bricks = lax.broadcasted_iota(jnp.int32, (count, blocks.shape[1]), 0).astype(F32) + float(first)
    hit = jnp.where(bricks == target, 1.0, 0.0).astype(BF16)
    return dot2(blocks, hit, NT)


def near_kernel(own, got_d, ng_low, ng, mass, near, inner):
    near[...] = brick_sums((own, got_d))
    for x in range(8):
        for a in range(8):
            low, high = x * NROW + a * 17, x * NROW + (a - 4) * 17
            if a < 4:
                inner[x, a] = ng_low[low : low + 16, :]
            elif a == 4:
                inner[x, a] = ng_low[low : low + 16, :] + ng[high : high + 16, :]
            else:
                inner[x, a] = ng[high : high + 16, :]
    for a in range(8):
        inner[8, a] = mass[a * 17 : a * 17 + 16, :]


def final_kernel(
    fields, wave_old, adj_old, src, adj_src, inner, near, got_s, got_d, got_sd,
    wave_next, adj_next, bricks, wave_buf, adj_buf, brick_buf, sem,
):
    keep_s = (lax.axis_index("surf") > 0).astype(F32)
    keep_d = (lax.axis_index("depth") > 0).astype(F32)
    first = lax.broadcasted_iota(jnp.int32, (16, 128), 0) == 0

    def total(ch, a):
        part = inner[ch, a]
        line = got_d[256 + ch * 8 + a : 257 + ch * 8 + a, :] * keep_d
        if a == 0:
            part = part + got_s[256 + ch * 16 : 272 + ch * 16, :] * keep_s
            line = line + got_sd[256 + ch : 257 + ch, :] * (keep_s * keep_d)
        return part + jnp.where(first, line, 0.0)

    for a in range(8):
        scale = (DT * DT) / total(8, a)
        for t in range(4):
            at = slice(t * PLANE + a * 16, t * PLANE + a * 16 + 16)
            now = slice(t * COLUMN + a * 16, t * COLUMN + a * 16 + 16)
            adj = slice(now.start + 4 * COLUMN, now.stop + 4 * COLUMN)
            wave_buf[at, :] = 2.0 * fields[now, :] - wave_old[at, :] + (src[at, :] - total(t, a)) * scale
            adj_buf[at, :] = (
                2.0 * fields[adj, :] - adj_old[at, :] + (adj_src[at, :] - total(4 + t, a)) * scale
            )
    copies = [
        pltpu.make_async_copy(wave_buf, wave_next, sem.at[0]),
        pltpu.make_async_copy(adj_buf, adj_next, sem.at[1]),
    ]
    for c in copies:
        c.start()
    for k in range(CHUNKS):
        cols = slice(k * (1024 // CHUNKS), (k + 1) * (1024 // CHUNKS))
        acc = near[:, cols] + brick_sums((got_s, got_sd), k * (1024 // CHUNKS), 1024 // CHUNKS)
        brick_buf[:, cols] = acc[0:125, :]
        copy = pltpu.make_async_copy(brick_buf.at[:, cols], bricks.at[:, cols], sem.at[2 + k])
        copy.start()
        copies.append(copy)
    for c in copies:
        c.wait()


def vmem(*shape):
    return pltpu.VMEM(shape, F32)


def out(*shape, dtype=F32):
    return jax.ShapeDtypeStruct(shape, dtype)


def send(x, ds, dd, wrap_s, wrap_d):
    ns, nd = lax.axis_size("surf"), lax.axis_size("depth")
    pairs = [
        (s * nd + d, (s + ds) % ns * nd + (d + dd) % nd)
        for s in range(ns)
        for d in range(nd)
        if (wrap_s or 0 <= s + ds < ns) and (wrap_d or 0 <= d + dd < nd)
    ]
    return lax.ppermute(x, ("surf", "depth"), pairs)


def call(kernel, name, ins, outs, scratch=(), specs=None, out_space=pltpu.VMEM):
    here = pl.BlockSpec(memory_space=pltpu.VMEM)
    return pl.pallas_call(
        kernel,
        out_shape=tuple(outs),
        in_specs=specs or [here] * len(ins),
        out_specs=tuple(pl.BlockSpec(memory_space=out_space) for _ in outs),
        scratch_shapes=list(scratch),
        compiler_params=pltpu.CompilerParams(vmem_limit_bytes=48 * 1024 * 1024),
        name=name,
    )(*ins)


def in_hbm(x):
    return pltpu.with_memory_space_constraint(x, pltpu.HBM)


def per_device(
    wave_now, wave_old, adj_now, adj_old, source, adj_source,
    inv_density, inv_modulus, element_cell, send_elem, send_brick, send_count,
):
    shape = wave_now.shape
    wave, wave_old, adj, adj_old, source, adj_source = (
        x.reshape(4 * PLANE, 128)
        for x in (wave_now, wave_old, adj_now, adj_old, source, adj_source)
    )
    there = pl.BlockSpec(memory_space=pltpu.HBM)
    line, plane = call(
        pack_kernel, "pack", [in_hbm(x) for x in (wave_now, adj_now)], (out(8, 8, 128), out(8, 16, 128)),
        [pltpu.SemaphoreType.DMA((4,))], [there] * 2,
    )
    hc = send(line, 0, -1, True, True)
    prep = call(
        prep_kernel,
        "prep",
        [in_hbm(x) for x in (wave, adj, inv_density, inv_modulus, element_cell, send_elem, send_brick, send_count)],
        (out(8 * COLUMN, 128), out(128, 256), out(160, 128), out(8, 256),
         out(512, 512, dtype=BF16), out(512, 512, dtype=BF16), out(128, 128)),
        [vmem(125, 256), vmem(125, 256), pltpu.VMEM((1, 256), jnp.int32),
         pltpu.VMEM((1, 4, 256), jnp.int32), pltpu.VMEM((1, 4, 256), jnp.int32),
         pltpu.SMEM((1, 4), jnp.int32), pltpu.SemaphoreType.DMA((14,)), vmem(160, 128), vmem(160, 128), vmem(64, 512)],
        [there] * 8,
    )
    hc, plane, prep = lax.optimization_barrier((hc, plane, tuple(prep)))
    fields, stiff, mass, targ, spread, fold, wcol = prep
    ha = send(jnp.concatenate([plane.reshape(128, 128), hc[:, 0]], 0), -1, 0, True, True)

    kern_low, ng_low, val_up, prod_up, frc_up = call(
        early_kernel,
        "early",
        (fields, hc.reshape(64, 128), stiff, spread, fold, wcol),
        (out(128, 128), out(8 * NROW, 128), out(160, 640), out(800, 128), out(160, 640)),
        [vmem(200, 512), vmem(200, 640), vmem(1000, 128), vmem(200, 640)],
    )
    ng, own, buf_s, buf_d, buf_sd = call(
        late_kernel,
        "late",
        (ha, stiff, spread, fold, wcol, kern_low, ng_low, mass, targ, val_up, prod_up, frc_up),
        (out(8 * NROW, 128), out(256, 128), out(400, 128), out(328, 128), out(272, 128)),
        [vmem(128, 128), vmem(200, 512), vmem(40, 640),
         vmem(1000, 128), vmem(200, 640)],
    )
    got_s = send(buf_s, 1, 0, True, True)
    got_d = send(buf_d, 0, 1, True, True)
    got_sd = send(buf_sd, 1, 1, False, False)
    near, inner = call(
        near_kernel, "near", (own, got_d, ng_low, ng, mass), (out(128, 1024), out(9, 8, 16, 128))
    )
    wave_next, adj_next, bricks = call(
        final_kernel,
        "final",
        (fields, wave_old, adj_old, source, adj_source, inner, near, got_s, got_d, got_sd),
        (out(4 * PLANE, 128), out(4 * PLANE, 128), out(125, 1024)),
        [vmem(4 * PLANE, 128), vmem(4 * PLANE, 128), vmem(125, 1024), pltpu.SemaphoreType.DMA((2 + CHUNKS,))],
        out_space=pl.ANY,
    )
    return wave_next.reshape(shape), adj_next.reshape(shape), bricks


def solution(mesh):
    field = P(None, "surf", "depth", None)
    both = ("surf", "depth")
    return jax.shard_map(
        per_device,
        mesh=mesh,
        in_specs=(field,) * 6
        + (P(None, both), P(None, both), P(both, None), P(both, None, None), P(both, None, None), P(both, None)),
        out_specs=(field, field, P(None, both)),
        check_vma=False,
    )
```

```python
import math

import jax
import jax.numpy as jnp
import numpy as np
from jax import lax
from jax.experimental import pallas as pl
from jax.experimental.pallas import tpu as pltpu
from jax.sharding import PartitionSpec as P

F32 = jnp.float32
BF16 = jnp.bfloat16
DT = 0.05
NT = (((1,), (1,)), ((), ()))
CHUNKS = 2
NROW = 85
COLUMN = 136
PLANE = 128


def gll():
    x = np.array([-1.0, -math.sqrt(3.0 / 7.0), 0.0, math.sqrt(3.0 / 7.0), 1.0])
    w = np.array([0.1, 49.0 / 90.0, 32.0 / 45.0, 49.0 / 90.0, 0.1])
    eye = np.eye(5)
    diff = x[:, None] - x[None, :] + eye
    prod = np.prod(diff, axis=1)
    deriv = prod[:, None] / prod[None, :] / diff
    inv = np.where(eye > 0.5, 0.0, 1.0 / diff)
    deriv = np.where(eye > 0.5, inv.sum(axis=1)[:, None], deriv)
    return deriv, w


DERIV, WEIGHT = gll()


def apply_deriv(mat, v):
    e0, e1, e2 = v[0] + v[4], v[1] + v[3], v[2]
    o0, o1 = v[0] - v[4], v[1] - v[3]
    half = lambda i, l: float(0.5 * (mat[i, l] + mat[i, 4 - l]))
    dif = lambda i, l: float(0.5 * (mat[i, l] - mat[i, 4 - l]))
    odd = [half(i, 0) * e0 + half(i, 1) * e1 + float(mat[i, 2]) * e2 for i in (0, 1)]
    even = [dif(i, 0) * o0 + dif(i, 1) * o1 for i in (0, 1, 2)]
    return [even[0] + odd[0], even[1] + odd[1], even[2], even[1] - odd[1], even[0] - odd[0]]


def split2(x):
    hi = x.astype(BF16)
    return hi, (x - hi.astype(F32)).astype(BF16)


def dot2(x, table, dims=(((1,), (0,)), ((), ()))):
    hi, lo = split2(x)
    rows = x.shape[0]
    if rows % 16 == 0:
        both = jnp.concatenate([hi, lo], axis=0)
        both = lax.dot_general(both, table, dims, preferred_element_type=F32)
        return both[0:rows] + both[rows:]
    return lax.dot_general(hi, table, dims, preferred_element_type=F32) + lax.dot_general(
        lo, table, dims, preferred_element_type=F32
    )


def pack_kernel(wave, adj, line, plane, sem):
    copies = []
    for k, src in enumerate((wave, adj)):
        to = pl.ds(4 * k, 4)
        copies.append(pltpu.make_async_copy(src.at[:, :, 0, :], line.at[to], sem.at[2 * k]))
        copies.append(pltpu.make_async_copy(src.at[:, 0], plane.at[to], sem.at[2 * k + 1]))
    for c in copies:
        c.start()
    for c in copies:
        c.wait()


def prep_kernel(
    wave_hbm, adj_hbm, dens_hbm, modu_hbm, cell_hbm, selem_hbm, sbrick_hbm, scount_hbm,
    fields, stiff, mass, targ, spread, fold, wcol,
    dens, modu, cell, selem, sbrick, scount, sem, ms0, ms1, mo,
):
    pairs = (
        (dens_hbm, dens), (modu_hbm, modu), (cell_hbm, cell), (selem_hbm, selem), (sbrick_hbm, sbrick),
        (scount_hbm, scount),
    )
    copies = [pltpu.make_async_copy(a, b, sem.at[k]) for k, (a, b) in enumerate(pairs)]
    late_copies = []
    for x in range(8):
        src = (wave_hbm if x < 4 else adj_hbm).at[pl.ds(x % 4 * PLANE, PLANE)]
        late_copies.append(pltpu.make_async_copy(src, fields.at[pl.ds(x * COLUMN, PLANE)], sem.at[6 + x]))
    for c in copies + late_copies:
        c.start()
    sub = lax.broadcasted_iota(jnp.int32, (128, 128), 0)
    lane = lax.broadcasted_iota(jnp.int32, (128, 128), 1)
    fold[...] = jnp.zeros(fold.shape, BF16)
    for r in range(4):
        node = (4 * (lane & 31) + r) & 127
        hit = sub == node
        for ec in range(4):
            spread[ec * 128 : ec * 128 + 128, r * 128 : r * 128 + 128] = jnp.where(
                hit & ((lane >> 5) == ec), 1.0, 0.0
            ).astype(BF16)
        back = jnp.where(lane == ((4 * (sub & 31) + r) & 127), 1.0, 0.0).astype(BF16)
        for ec in range(4):
            rows = slice(r * 128 + ec * 32, r * 128 + ec * 32 + 32)
            fold[rows, ec * 128 : ec * 128 + 128] = back[ec * 32 : ec * 32 + 32]

    def weight(i):
        edge = float(WEIGHT[0])
        return jnp.where(
            i == 2, float(WEIGHT[2]), jnp.where((i == 0) | (i == 4), edge, float(WEIGHT[1]))
        )

    p = (sub >= 25).astype(jnp.int32) + (sub >= 50) + (sub >= 75) + (sub >= 100) + (sub >= 125)
    rest = sub - 25 * p
    q = (rest >= 5).astype(jnp.int32) + (rest >= 10) + (rest >= 15) + (rest >= 20)
    cub = weight(p) * weight(q) * weight(rest - 5 * q)
    wcol[...] = cub * -DT
    for c in copies:
        c.wait()
    both = jnp.concatenate([cub[0:125], cub[0:125]], axis=1)
    place = (lax.broadcasted_iota(jnp.int32, (256, 256), 0) == cell[...]).astype(F32).astype(BF16)
    stiff[0:125, :] = dot2(dens[...], place, NT) * both
    cells = dot2(modu[...], place, NT) * both
    mass[...] = jnp.zeros(mass.shape, F32)
    lined = []
    for ea, ms in ((0, ms0), (1, ms1)):
        ms[0:125, :] = cells[:, ea * 128 : ea * 128 + 128]
        ms[125:160, :] = jnp.zeros((35, 128), F32)
        parts = [ms[pl.ds(r, 32, stride=5), :] for r in range(5)]
        parts[0] = parts[0] + to_next(parts.pop())
        lined.append(jnp.concatenate(parts, axis=1))
    mo[...] = dot2(jnp.concatenate(lined, axis=0), fold[...])
    for ea in range(2):
        for p in range(5):
            for ec in range(4):
                at = pl.ds((4 * ea + p) * 17 + 4 * ec, 5)
                row = ea * 32 + p * 5
                mass[at, :] = mass[at, :] + mo[row : row + 5, ec * 128 : ec * 128 + 128]
    sub = lax.broadcasted_iota(jnp.int32, (8, 256), 0)
    lane = lax.broadcasted_iota(jnp.int32, (1, 256), 1)
    elem_iota = lax.broadcasted_iota(jnp.int32, (256, 256), 0)
    acc = jnp.zeros((8, 256), F32)
    for t in range(4):
        brick = jnp.where(lane < scount[0, t], sbrick[0, t : t + 1, :] + 1, 0)
        high = lax.shift_right_logical(brick, 5)
        low = brick - high * 32
        rows = jnp.where(sub == t, high, jnp.where(sub == t + 4, low, 0))
        pick = (elem_iota == selem[0, t : t + 1, :]).astype(F32).astype(BF16)
        acc = acc + lax.dot_general(
            rows.astype(F32).astype(BF16), pick, NT, preferred_element_type=F32
        )
    at_cell = lax.dot_general(acc.astype(BF16), place, NT, preferred_element_type=F32)
    targ[0:4, :] = 32.0 * at_cell[0:4] + at_cell[4:8] - 1.0
    for c in late_copies:
        c.wait()


def load_plane(row_of, lhs, row):
    for c in range(17):
        tile = row_of(c)
        if c < 16:
            at = row + c % 4 * 8
            lhs[at : at + 8, c // 4 * 128 : c // 4 * 128 + 128] = tile
        if c % 4 == 0 and c > 0:
            lhs[row + 32 : row + 40, (c // 4 - 1) * 128 : c // 4 * 128] = tile


def from_next(x):
    last = (lax.broadcasted_iota(jnp.int32, x.shape, 1) & 31) == 31
    return jnp.where(last, pltpu.roll(x, 31, 1), pltpu.roll(x, 127, 1))


def to_next(x):
    zeroth = (lax.broadcasted_iota(jnp.int32, x.shape, 1) & 31) == 0
    return jnp.where(zeroth, pltpu.roll(x, 97, 1), pltpu.roll(x, 1, 1))


def spread_planes(val, row, planes, spread):
    nodes = dot2(planes, spread[...])
    val[row : row + planes.shape[0], 0:512] = nodes
    val[row : row + planes.shape[0], 512:640] = from_next(nodes[:, 0:128])


def node_tile(p, q, r):
    return (slice((p * 5 + q) * 8, (p * 5 + q) * 8 + 8), slice(r * 128, r * 128 + 128))


def node_rows(p, q, r):
    at = (p * 25 + q * 5 + r) * 8
    return slice(at, at + 8)


def line_terms(ea, nodes, values, stiff):
    lanes = slice(ea * 128, ea * 128 + 128)
    grad = apply_deriv(DERIV, values)
    flux = []
    for k, (p, q, r) in enumerate(nodes):
        at = p * 25 + q * 5 + r
        flux.append(grad[k] * stiff[at : at + 1, lanes])
    return [g * pltpu.roll(g, 4, 0) for g in grad], apply_deriv(DERIV.T, flux)


def inside_plane(ea, p, val, at, stiff, prod, frc):
    for i in range(5):
        nodes = [(p, k, i) for k in range(5)]
        pair, force = line_terms(ea, nodes, [val[node_tile(at, k, i)] for k in range(5)], stiff)
        for k, n in enumerate(nodes):
            prod[node_rows(*n), :] = pair[k]
            frc[node_tile(*n)] = force[k]
    for i in range(5):
        nodes = [(p, i, k) for k in range(5)]
        pair, force = line_terms(ea, nodes, [val[node_tile(at, i, k)] for k in range(5)], stiff)
        for k, n in enumerate(nodes):
            prod[node_rows(*n), :] = prod[node_rows(*n), :] + pair[k]
            frc[node_tile(*n)] = frc[node_tile(*n)] + force[k]


def across_planes(ea, val, last, stiff, prod_in, frc_in, prod, frc):
    for q in range(5):
        for r in range(5):
            nodes = [(k, q, r) for k in range(5)]
            values = [val[node_tile(k, q, r)] for k in range(4)] + [last(q, r)]
            pair, force = line_terms(ea, nodes, values, stiff)
            for k, n in enumerate(nodes):
                old_p, old_f = (prod_in, frc_in) if k < 4 else (prod, frc)
                prod[node_rows(*n), :] = old_p[node_rows(*n), :] + pair[k]
                frc[node_tile(*n)] = old_f[node_tile(*n)] + force[k]


def finish_layer(prod, frc, lhs, fold, wcol, kern, ng):
    for j in range(16):
        count = 8 if j < 15 else 5
        total = sum(prod[pl.ds(j * 64 + t, count, stride=8), :] for t in range(4))
        kern[j * 8 : j * 8 + count, :] = total * wcol[j * 8 : j * 8 + count, :]
    kern[125:128, :] = jnp.zeros((3, 128), F32)
    zeroth = frc[:, 0:128] + to_next(frc[:, 512:640])
    lhs[...] = dot2(jnp.concatenate([zeroth, frc[:, 128:512]], axis=1), fold[...])
    for p in range(5):
        for c in range(17):
            parts = []
            if c < 16:
                at = (p * 5 + c % 4) * 8
                parts.append(lhs[at : at + 8, c // 4 * 128 : c // 4 * 128 + 128])
            if c % 4 == 0 and c > 0:
                at = (p * 5 + 4) * 8
                parts.append(lhs[at : at + 8, (c // 4 - 1) * 128 : c // 4 * 128])
            ng[pl.ds(p * 17 + c, 8, stride=NROW), :] = sum(parts)


def early_kernel(
    fields, hc, stiff, spread, fold, wcol, kern, ng, val_up, prod_up, frc_up, lhs, val, prod, frc
):
    keep = (lax.axis_index("depth") < lax.axis_size("depth") - 1).astype(F32)

    def field_row(a):
        def row_of(c):
            if c == 16:
                return hc[pl.ds(a, 8, stride=8), :] * keep
            return fields[pl.ds(a * 16 + c, 8, stride=COLUMN), :]

        return row_of

    for a in range(5):
        load_plane(field_row(a), lhs, a * 40)
    spread_planes(val, 0, lhs[...], spread)
    for p in range(5):
        inside_plane(0, p, val, p, stiff, prod, frc)
    across_planes(0, val, lambda q, r: val[node_tile(4, q, r)], stiff, prod, frc, prod, frc)
    finish_layer(prod, frc, lhs, fold, wcol, kern, ng)
    val_up[0:40, :] = val[160:200, :]
    for a in range(5, 8):
        load_plane(field_row(a), lhs, (a - 5) * 40)
    spread_planes(val_up, 40, lhs[0:120, :], spread)
    for p in range(4):
        inside_plane(1, p, val_up, p, stiff, prod_up, frc_up)


def late_kernel(
    ha, stiff, spread, fold, wcol, kern_low, ng_low, mass, targ, val_up, prod_up, frc_up,
    ng, own, buf_s, buf_d, buf_sd, kern, lhs, val, prod, frc,
):
    keep_d = (lax.axis_index("depth") < lax.axis_size("depth") - 1).astype(F32)
    keep_s = (lax.axis_index("surf") < lax.axis_size("surf") - 1).astype(F32)

    def row_of(c):
        if c == 16:
            return ha[128:136, :] * (keep_s * keep_d)
        return ha[pl.ds(c, 8, stride=16), :] * keep_s

    load_plane(row_of, lhs, 0)
    spread_planes(val, 0, lhs[0:40, :], spread)
    inside_plane(1, 4, val, 0, stiff, prod, frc)
    across_planes(1, val_up, lambda q, r: val[node_tile(0, q, r)], stiff, prod_up, frc_up, prod, frc)
    finish_layer(prod, frc, lhs, fold, wcol, kern, ng)
    for row, buf in ((0, own), (1, buf_s), (2, buf_d), (3, buf_sd)):
        buf[0:128, :] = kern_low[...]
        buf[128:256, :] = kern[...]
        buf[125:126, :] = targ[row : row + 1, 0:128]
        buf[253:254, :] = targ[row : row + 1, 128:256]
    for x in range(8):
        base = x * NROW
        for a in range(8):
            at = base + a * 17 + 16
            if a < 4:
                row = ng_low[at : at + 1, :]
            elif a == 4:
                row = ng_low[at : at + 1, :] + ng[base + 16 : base + 17, :]
            else:
                row = ng[at - 68 : at - 67, :]
            buf_d[256 + x * 8 + a : 257 + x * 8 + a, :] = row
        buf_s[256 + x * 16 : 272 + x * 16, :] = ng[base + 68 : base + 84, :]
        buf_sd[256 + x : 257 + x, :] = ng[base + 84 : base + 85, :]
    for a in range(8):
        buf_d[320 + a : 321 + a, :] = mass[a * 17 + 16 : a * 17 + 17, :]
    buf_s[384:400, :] = mass[136:152, :]
    buf_sd[264:265, :] = mass[152:153, :]
    buf_sd[265:272, :] = jnp.zeros((7, 128), F32)


def brick_sums(bufs, first=0, count=1024):
    blocks = jnp.concatenate([buf[at : at + 128, :] for buf in bufs for at in (0, 128)], axis=1)
    target = blocks[125:126, :]
    bricks = lax.broadcasted_iota(jnp.int32, (count, blocks.shape[1]), 0).astype(F32) + float(first)
    hit = jnp.where(bricks == target, 1.0, 0.0).astype(BF16)
    return dot2(blocks, hit, NT)


def stepped(now, before, src, force, scale):
    return 2.0 * now - before + (src - force) * scale


def near_kernel(
    own, got_d, ng_low, ng, mass, fields, wave_old, adj_old, src, adj_src,
    near, edge, wave_next, adj_next, wave_buf, adj_buf, sem,
):
    keep_d = (lax.axis_index("depth") > 0).astype(F32)
    first = lax.broadcasted_iota(jnp.int32, (16, 128), 0) == 0

    def total(ch, a):
        if ch == 8:
            part = mass[a * 17 : a * 17 + 16, :]
        else:
            low, high = ch * NROW + a * 17, ch * NROW + (a - 4) * 17
            part = ng_low[low : low + 16, :] if a <= 4 else ng[high : high + 16, :]
            if a == 4:
                part = part + ng[high : high + 16, :]
        line = got_d[256 + ch * 8 + a : 257 + ch * 8 + a, :] * keep_d
        return part + jnp.where(first, line, 0.0)

    for ch in range(9):
        edge[ch] = total(ch, 0)
    for a in range(1, 8):
        scale = (DT * DT) / total(8, a)
        for t in range(4):
            at = slice(t * PLANE + a * 16, t * PLANE + a * 16 + 16)
            now = slice(t * COLUMN + a * 16, t * COLUMN + a * 16 + 16)
            adj = slice(now.start + 4 * COLUMN, now.stop + 4 * COLUMN)
            wave_buf[at, :] = stepped(fields[now, :], wave_old[at, :], src[at, :], total(t, a), scale)
            adj_buf[at, :] = stepped(
                fields[adj, :], adj_old[at, :], adj_src[at, :], total(4 + t, a), scale
            )
    copies = []
    for t in range(4):
        rows = pl.ds(t * PLANE + 16, PLANE - 16)
        for k, (buf, to) in enumerate(((wave_buf, wave_next), (adj_buf, adj_next))):
            copies.append(pltpu.make_async_copy(buf.at[rows], to.at[rows], sem.at[2 * t + k]))
    for c in copies:
        c.start()
    near[...] = brick_sums((own, got_d))
    for c in copies:
        c.wait()


def final_kernel(
    fields, wave_old, adj_old, src, adj_src, edge, near, got_s, got_sd, wave_in, adj_in,
    wave_next, adj_next, bricks, wave_buf, adj_buf, brick_buf, sem,
):
    keep_s = (lax.axis_index("surf") > 0).astype(F32)
    keep_d = (lax.axis_index("depth") > 0).astype(F32)
    first = lax.broadcasted_iota(jnp.int32, (16, 128), 0) == 0

    def total(ch):
        line = got_sd[256 + ch : 257 + ch, :] * (keep_s * keep_d)
        plane = got_s[256 + ch * 16 : 272 + ch * 16, :] * keep_s
        return edge[ch] + plane + jnp.where(first, line, 0.0)

    scale = (DT * DT) / total(8)
    copies = []
    for t in range(4):
        at = slice(t * PLANE, t * PLANE + 16)
        now = slice(t * COLUMN, t * COLUMN + 16)
        adj = slice(now.start + 4 * COLUMN, now.stop + 4 * COLUMN)
        wave_buf[t] = stepped(fields[now, :], wave_old[at, :], src[at, :], total(t), scale)
        adj_buf[t] = stepped(fields[adj, :], adj_old[at, :], adj_src[at, :], total(4 + t), scale)
        rows = pl.ds(t * PLANE, 16)
        for k, (buf, to) in enumerate(((wave_buf, wave_next), (adj_buf, adj_next))):
            copies.append(pltpu.make_async_copy(buf.at[t], to.at[rows], sem.at[2 * t + k]))
    for c in copies:
        c.start()
    for k in range(CHUNKS):
        cols = slice(k * (1024 // CHUNKS), (k + 1) * (1024 // CHUNKS))
        acc = near[:, cols] + brick_sums((got_s, got_sd), k * (1024 // CHUNKS), 1024 // CHUNKS)
        brick_buf[:, cols] = acc[0:125, :]
        copy = pltpu.make_async_copy(brick_buf.at[:, cols], bricks.at[:, cols], sem.at[8 + k])
        copy.start()
        copies.append(copy)
    for c in copies:
        c.wait()


def vmem(*shape):
    return pltpu.VMEM(shape, F32)


def out(*shape, dtype=F32):
    return jax.ShapeDtypeStruct(shape, dtype)


def send(x, ds, dd, wrap_s, wrap_d):
    ns, nd = lax.axis_size("surf"), lax.axis_size("depth")
    pairs = [
        (s * nd + d, (s + ds) % ns * nd + (d + dd) % nd)
        for s in range(ns)
        for d in range(nd)
        if (wrap_s or 0 <= s + ds < ns) and (wrap_d or 0 <= d + dd < nd)
    ]
    return lax.ppermute(x, ("surf", "depth"), pairs)


def call(kernel, name, ins, outs, scratch=(), specs=None, out_spaces=None, aliases=()):
    here = pl.BlockSpec(memory_space=pltpu.VMEM)
    spaces = out_spaces or [pltpu.VMEM] * len(outs)
    return pl.pallas_call(
        kernel,
        out_shape=tuple(outs),
        in_specs=specs or [here] * len(ins),
        out_specs=tuple(pl.BlockSpec(memory_space=space) for space in spaces),
        scratch_shapes=list(scratch),
        input_output_aliases=dict(aliases),
        compiler_params=pltpu.CompilerParams(vmem_limit_bytes=48 * 1024 * 1024),
        name=name,
    )(*ins)


def in_hbm(x):
    return pltpu.with_memory_space_constraint(x, pltpu.HBM)


def per_device(
    wave_now, wave_old, adj_now, adj_old, source, adj_source,
    inv_density, inv_modulus, element_cell, send_elem, send_brick, send_count,
):
    shape = wave_now.shape
    wave, wave_old, adj, adj_old, source, adj_source = (
        x.reshape(4 * PLANE, 128)
        for x in (wave_now, wave_old, adj_now, adj_old, source, adj_source)
    )
    there = pl.BlockSpec(memory_space=pltpu.HBM)
    line, plane = call(
        pack_kernel, "pack", [in_hbm(x) for x in (wave_now, adj_now)], (out(8, 8, 128), out(8, 16, 128)),
        [pltpu.SemaphoreType.DMA((4,))], [there] * 2,
    )
    hc = send(line, 0, -1, True, True)
    prep = call(
        prep_kernel,
        "prep",
        [in_hbm(x) for x in (wave, adj, inv_density, inv_modulus, element_cell, send_elem, send_brick, send_count)],
        (out(8 * COLUMN, 128), out(128, 256), out(160, 128), out(8, 256),
         out(512, 512, dtype=BF16), out(512, 512, dtype=BF16), out(128, 128)),
        [vmem(125, 256), vmem(125, 256), pltpu.VMEM((1, 256), jnp.int32),
         pltpu.VMEM((1, 4, 256), jnp.int32), pltpu.VMEM((1, 4, 256), jnp.int32),
         pltpu.SMEM((1, 4), jnp.int32), pltpu.SemaphoreType.DMA((14,)), vmem(160, 128), vmem(160, 128), vmem(64, 512)],
        [there] * 8,
    )
    hc, plane, prep = lax.optimization_barrier((hc, plane, tuple(prep)))
    fields, stiff, mass, targ, spread, fold, wcol = prep
    ha = send(jnp.concatenate([plane.reshape(128, 128), hc[:, 0]], 0), -1, 0, True, True)

    kern_low, ng_low, val_up, prod_up, frc_up = call(
        early_kernel,
        "early",
        (fields, hc.reshape(64, 128), stiff, spread, fold, wcol),
        (out(128, 128), out(8 * NROW, 128), out(160, 640), out(800, 128), out(160, 640)),
        [vmem(200, 512), vmem(200, 640), vmem(1000, 128), vmem(200, 640)],
    )
    ng, own, buf_s, buf_d, buf_sd = call(
        late_kernel,
        "late",
        (ha, stiff, spread, fold, wcol, kern_low, ng_low, mass, targ, val_up, prod_up, frc_up),
        (out(8 * NROW, 128), out(256, 128), out(400, 128), out(328, 128), out(272, 128)),
        [vmem(128, 128), vmem(200, 512), vmem(40, 640),
         vmem(1000, 128), vmem(200, 640)],
    )
    got_s = send(buf_s, 1, 0, True, True)
    got_d = send(buf_d, 0, 1, True, True)
    got_sd = send(buf_sd, 1, 1, False, False)
    field = out(4 * PLANE, 128)
    rest = (fields, wave_old, adj_old, source, adj_source)
    near, edge, wave_part, adj_part = call(
        near_kernel,
        "near",
        (own, got_d, ng_low, ng, mass) + rest,
        (out(128, 1024), out(9, 16, 128), field, field),
        [vmem(4 * PLANE, 128), vmem(4 * PLANE, 128), pltpu.SemaphoreType.DMA((8,))],
        out_spaces=[pltpu.VMEM, pltpu.VMEM, pltpu.HBM, pltpu.HBM],
    )
    wave_next, adj_next, bricks = call(
        final_kernel,
        "final",
        rest + (edge, near, got_s, got_sd, wave_part, adj_part),
        (field, field, out(125, 1024)),
        [vmem(4, 16, 128), vmem(4, 16, 128), vmem(125, 1024), pltpu.SemaphoreType.DMA((8 + CHUNKS,))],
        [pl.BlockSpec(memory_space=pltpu.VMEM)] * 9 + [there] * 2,
        [pltpu.HBM, pltpu.HBM, pl.ANY],
        ((9, 0), (10, 1)),
    )
    return wave_next.reshape(shape), adj_next.reshape(shape), bricks


def solution(mesh):
    field = P(None, "surf", "depth", None)
    both = ("surf", "depth")
    return jax.shard_map(
        per_device,
        mesh=mesh,
        in_specs=(field,) * 6
        + (P(None, both), P(None, both), P(both, None), P(both, None, None), P(both, None, None), P(both, None)),
        out_specs=(field, field, P(None, both)),
        check_vma=False,
    )
```

```python
import math

import jax
import jax.numpy as jnp
import numpy as np
from jax import lax
from jax.experimental import pallas as pl
from jax.experimental.pallas import tpu as pltpu
from jax.sharding import PartitionSpec as P

F32 = jnp.float32
BF16 = jnp.bfloat16
DT = 0.05
NT = (((1,), (1,)), ((), ()))
CHUNKS = 2
NROW = 85
COLUMN = 136
PLANE = 128


def gll():
    x = np.array([-1.0, -math.sqrt(3.0 / 7.0), 0.0, math.sqrt(3.0 / 7.0), 1.0])
    w = np.array([0.1, 49.0 / 90.0, 32.0 / 45.0, 49.0 / 90.0, 0.1])
    eye = np.eye(5)
    diff = x[:, None] - x[None, :] + eye
    prod = np.prod(diff, axis=1)
    deriv = prod[:, None] / prod[None, :] / diff
    inv = np.where(eye > 0.5, 0.0, 1.0 / diff)
    deriv = np.where(eye > 0.5, inv.sum(axis=1)[:, None], deriv)
    return deriv, w


DERIV, WEIGHT = gll()


def apply_deriv(mat, v):
    e0, e1, e2 = v[0] + v[4], v[1] + v[3], v[2]
    o0, o1 = v[0] - v[4], v[1] - v[3]
    half = lambda i, l: float(0.5 * (mat[i, l] + mat[i, 4 - l]))
    dif = lambda i, l: float(0.5 * (mat[i, l] - mat[i, 4 - l]))
    odd = [half(i, 0) * e0 + half(i, 1) * e1 + float(mat[i, 2]) * e2 for i in (0, 1)]
    even = [dif(i, 0) * o0 + dif(i, 1) * o1 for i in (0, 1, 2)]
    return [even[0] + odd[0], even[1] + odd[1], even[2], even[1] - odd[1], even[0] - odd[0]]


def split2(x):
    hi = x.astype(BF16)
    return hi, (x - hi.astype(F32)).astype(BF16)


def dot2(x, table, dims=(((1,), (0,)), ((), ()))):
    hi, lo = split2(x)
    rows = x.shape[0]
    if rows % 16 == 0:
        both = jnp.concatenate([hi, lo], axis=0)
        both = lax.dot_general(both, table, dims, preferred_element_type=F32)
        return both[0:rows] + both[rows:]
    return lax.dot_general(hi, table, dims, preferred_element_type=F32) + lax.dot_general(
        lo, table, dims, preferred_element_type=F32
    )


def pack_kernel(wave, adj, line, plane, sem):
    copies = []
    for k, src in enumerate((wave, adj)):
        to = pl.ds(4 * k, 4)
        copies.append(pltpu.make_async_copy(src.at[:, :, 0, :], line.at[to], sem.at[2 * k]))
        copies.append(pltpu.make_async_copy(src.at[:, 0], plane.at[to], sem.at[2 * k + 1]))
    for c in copies:
        c.start()
    for c in copies:
        c.wait()


def prep_kernel(
    wave_hbm, adj_hbm, dens_hbm, modu_hbm, cell_hbm, selem_hbm, sbrick_hbm, scount_hbm,
    fields, stiff, mass, targ, spread, fold, wcol,
    dens, modu, cell, selem, sbrick, scount, sem, ms0, ms1, mo,
):
    pairs = (
        (dens_hbm, dens), (modu_hbm, modu), (cell_hbm, cell), (selem_hbm, selem), (sbrick_hbm, sbrick),
        (scount_hbm, scount),
    )
    copies = [pltpu.make_async_copy(a, b, sem.at[k]) for k, (a, b) in enumerate(pairs)]
    late_copies = []
    for x in range(8):
        src = (wave_hbm if x < 4 else adj_hbm).at[pl.ds(x % 4 * PLANE, PLANE)]
        late_copies.append(pltpu.make_async_copy(src, fields.at[pl.ds(x * COLUMN, PLANE)], sem.at[6 + x]))
    for c in copies + late_copies:
        c.start()
    sub = lax.broadcasted_iota(jnp.int32, (128, 128), 0)
    lane = lax.broadcasted_iota(jnp.int32, (128, 128), 1)
    fold[...] = jnp.zeros(fold.shape, BF16)
    for r in range(4):
        node = (4 * (lane & 31) + r) & 127
        hit = sub == node
        for ec in range(4):
            spread[ec * 128 : ec * 128 + 128, r * 128 : r * 128 + 128] = jnp.where(
                hit & ((lane >> 5) == ec), 1.0, 0.0
            ).astype(BF16)
        back = jnp.where(lane == ((4 * (sub & 31) + r) & 127), 1.0, 0.0).astype(BF16)
        for ec in range(4):
            rows = slice(r * 128 + ec * 32, r * 128 + ec * 32 + 32)
            fold[rows, ec * 128 : ec * 128 + 128] = back[ec * 32 : ec * 32 + 32]

    def weight(i):
        edge = float(WEIGHT[0])
        return jnp.where(
            i == 2, float(WEIGHT[2]), jnp.where((i == 0) | (i == 4), edge, float(WEIGHT[1]))
        )

    p = (sub >= 25).astype(jnp.int32) + (sub >= 50) + (sub >= 75) + (sub >= 100) + (sub >= 125)
    rest = sub - 25 * p
    q = (rest >= 5).astype(jnp.int32) + (rest >= 10) + (rest >= 15) + (rest >= 20)
    cub = weight(p) * weight(q) * weight(rest - 5 * q)
    wcol[...] = cub * -DT
    for c in copies:
        c.wait()
    both = jnp.concatenate([cub[0:125], cub[0:125]], axis=1)
    place = (lax.broadcasted_iota(jnp.int32, (256, 256), 0) == cell[...]).astype(F32).astype(BF16)
    stiff[0:125, :] = dot2(dens[...], place, NT) * both
    cells = dot2(modu[...], place, NT) * both
    mass[...] = jnp.zeros(mass.shape, F32)
    lined = []
    for ea, ms in ((0, ms0), (1, ms1)):
        ms[0:125, :] = cells[:, ea * 128 : ea * 128 + 128]
        ms[125:160, :] = jnp.zeros((35, 128), F32)
        parts = [ms[pl.ds(r, 32, stride=5), :] for r in range(5)]
        parts[0] = parts[0] + to_next(parts.pop())
        lined.append(jnp.concatenate(parts, axis=1))
    mo[...] = dot2(jnp.concatenate(lined, axis=0), fold[...])
    for ea in range(2):
        for p in range(5):
            for ec in range(4):
                at = pl.ds((4 * ea + p) * 17 + 4 * ec, 5)
                row = ea * 32 + p * 5
                mass[at, :] = mass[at, :] + mo[row : row + 5, ec * 128 : ec * 128 + 128]
    sub = lax.broadcasted_iota(jnp.int32, (8, 256), 0)
    lane = lax.broadcasted_iota(jnp.int32, (1, 256), 1)
    elem_iota = lax.broadcasted_iota(jnp.int32, (256, 256), 0)
    acc = jnp.zeros((8, 256), F32)
    for t in range(4):
        brick = jnp.where(lane < scount[0, t], sbrick[0, t : t + 1, :] + 1, 0)
        high = lax.shift_right_logical(brick, 5)
        low = brick - high * 32
        rows = jnp.where(sub == t, high, jnp.where(sub == t + 4, low, 0))
        pick = (elem_iota == selem[0, t : t + 1, :]).astype(F32).astype(BF16)
        acc = acc + lax.dot_general(
            rows.astype(F32).astype(BF16), pick, NT, preferred_element_type=F32
        )
    at_cell = lax.dot_general(acc.astype(BF16), place, NT, preferred_element_type=F32)
    targ[0:4, :] = 32.0 * at_cell[0:4] + at_cell[4:8] - 1.0
    for c in late_copies:
        c.wait()


def load_plane(row_of, lhs, row):
    for c in range(17):
        tile = row_of(c)
        if c < 16:
            at = row + c % 4 * 8
            lhs[at : at + 8, c // 4 * 128 : c // 4 * 128 + 128] = tile
        if c % 4 == 0 and c > 0:
            lhs[row + 32 : row + 40, (c // 4 - 1) * 128 : c // 4 * 128] = tile


def from_next(x):
    last = (lax.broadcasted_iota(jnp.int32, x.shape, 1) & 31) == 31
    return jnp.where(last, pltpu.roll(x, 31, 1), pltpu.roll(x, 127, 1))


def to_next(x):
    zeroth = (lax.broadcasted_iota(jnp.int32, x.shape, 1) & 31) == 0
    return jnp.where(zeroth, pltpu.roll(x, 97, 1), pltpu.roll(x, 1, 1))


def spread_planes(val, row, planes, spread):
    nodes = dot2(planes, spread[...])
    val[row : row + planes.shape[0], 0:512] = nodes
    val[row : row + planes.shape[0], 512:640] = from_next(nodes[:, 0:128])


def node_tile(p, q, r):
    return (slice((p * 5 + q) * 8, (p * 5 + q) * 8 + 8), slice(r * 128, r * 128 + 128))


def node_rows(p, q, r):
    at = (p * 25 + q * 5 + r) * 8
    return slice(at, at + 8)


def line_terms(ea, nodes, values, stiff):
    lanes = slice(ea * 128, ea * 128 + 128)
    grad = apply_deriv(DERIV, values)
    flux = []
    for k, (p, q, r) in enumerate(nodes):
        at = p * 25 + q * 5 + r
        flux.append(grad[k] * stiff[at : at + 1, lanes])
    return [g * pltpu.roll(g, 4, 0) for g in grad], apply_deriv(DERIV.T, flux)


def inside_plane(ea, p, val, at, stiff, prod, frc):
    for i in range(5):
        nodes = [(p, k, i) for k in range(5)]
        pair, force = line_terms(ea, nodes, [val[node_tile(at, k, i)] for k in range(5)], stiff)
        for k, n in enumerate(nodes):
            prod[node_rows(*n), :] = pair[k]
            frc[node_tile(*n)] = force[k]
    for i in range(5):
        nodes = [(p, i, k) for k in range(5)]
        pair, force = line_terms(ea, nodes, [val[node_tile(at, i, k)] for k in range(5)], stiff)
        for k, n in enumerate(nodes):
            prod[node_rows(*n), :] = prod[node_rows(*n), :] + pair[k]
            frc[node_tile(*n)] = frc[node_tile(*n)] + force[k]


def across_planes(ea, val, last, stiff, prod_in, frc_in, prod, frc):
    for q in range(5):
        for r in range(5):
            nodes = [(k, q, r) for k in range(5)]
            values = [val[node_tile(k, q, r)] for k in range(4)] + [last(q, r)]
            pair, force = line_terms(ea, nodes, values, stiff)
            for k, n in enumerate(nodes):
                old_p, old_f = (prod_in, frc_in) if k < 4 else (prod, frc)
                prod[node_rows(*n), :] = old_p[node_rows(*n), :] + pair[k]
                frc[node_tile(*n)] = old_f[node_tile(*n)] + force[k]


def finish_layer(prod, frc, lhs, fold, wcol, kern, ng):
    for j in range(16):
        count = 8 if j < 15 else 5
        total = sum(prod[pl.ds(j * 64 + t, count, stride=8), :] for t in range(4))
        kern[j * 8 : j * 8 + count, :] = total * wcol[j * 8 : j * 8 + count, :]
    kern[125:128, :] = jnp.zeros((3, 128), F32)
    zeroth = frc[:, 0:128] + to_next(frc[:, 512:640])
    lhs[...] = dot2(jnp.concatenate([zeroth, frc[:, 128:512]], axis=1), fold[...])
    for p in range(5):
        for c in range(17):
            parts = []
            if c < 16:
                at = (p * 5 + c % 4) * 8
                parts.append(lhs[at : at + 8, c // 4 * 128 : c // 4 * 128 + 128])
            if c % 4 == 0 and c > 0:
                at = (p * 5 + 4) * 8
                parts.append(lhs[at : at + 8, (c // 4 - 1) * 128 : c // 4 * 128])
            ng[pl.ds(p * 17 + c, 8, stride=NROW), :] = sum(parts)


def early_kernel(
    fields, hc, stiff, spread, fold, wcol, kern, ng, val_up, prod_up, frc_up, lhs, val, prod, frc
):
    keep = (lax.axis_index("depth") < lax.axis_size("depth") - 1).astype(F32)

    def field_row(a):
        def row_of(c):
            if c == 16:
                return hc[pl.ds(a, 8, stride=8), :] * keep
            return fields[pl.ds(a * 16 + c, 8, stride=COLUMN), :]

        return row_of

    for a in range(5):
        load_plane(field_row(a), lhs, a * 40)
    spread_planes(val, 0, lhs[...], spread)
    for p in range(5):
        inside_plane(0, p, val, p, stiff, prod, frc)
    across_planes(0, val, lambda q, r: val[node_tile(4, q, r)], stiff, prod, frc, prod, frc)
    finish_layer(prod, frc, lhs, fold, wcol, kern, ng)
    val_up[0:40, :] = val[160:200, :]
    for a in range(5, 8):
        load_plane(field_row(a), lhs, (a - 5) * 40)
    spread_planes(val_up, 40, lhs[0:120, :], spread)
    for p in range(4):
        inside_plane(1, p, val_up, p, stiff, prod_up, frc_up)


def late_kernel(
    ha, stiff, spread, fold, wcol, kern_low, ng_low, mass, targ, val_up, prod_up, frc_up,
    ng, kern, buf_s, lhs, val, prod, frc,
):
    keep_d = (lax.axis_index("depth") < lax.axis_size("depth") - 1).astype(F32)
    keep_s = (lax.axis_index("surf") < lax.axis_size("surf") - 1).astype(F32)

    def row_of(c):
        if c == 16:
            return ha[128:136, :] * (keep_s * keep_d)
        return ha[pl.ds(c, 8, stride=16), :] * keep_s

    load_plane(row_of, lhs, 0)
    spread_planes(val, 0, lhs[0:40, :], spread)
    inside_plane(1, 4, val, 0, stiff, prod, frc)
    across_planes(1, val_up, lambda q, r: val[node_tile(0, q, r)], stiff, prod_up, frc_up, prod, frc)
    finish_layer(prod, frc, lhs, fold, wcol, kern, ng)
    buf_s[0:128, :] = kern_low[...]
    buf_s[128:256, :] = kern[...]
    buf_s[125:126, :] = targ[1:2, 0:128]
    buf_s[253:254, :] = targ[1:2, 128:256]
    for x in range(8):
        base = x * NROW
        buf_s[256 + x * 16 : 272 + x * 16, :] = ng[base + 68 : base + 84, :]
    buf_s[384:400, :] = mass[136:152, :]


def pick_kernel(kern_low, kern, ng_low, ng, mass, targ, own, buf_d, buf_sd):
    for row, buf in ((0, own), (2, buf_d), (3, buf_sd)):
        buf[0:128, :] = kern_low[...]
        buf[128:256, :] = kern[...]
        buf[125:126, :] = targ[row : row + 1, 0:128]
        buf[253:254, :] = targ[row : row + 1, 128:256]
    for x in range(8):
        base = x * NROW
        for a in range(8):
            at = base + a * 17 + 16
            if a < 4:
                row = ng_low[at : at + 1, :]
            elif a == 4:
                row = ng_low[at : at + 1, :] + ng[base + 16 : base + 17, :]
            else:
                row = ng[at - 68 : at - 67, :]
            buf_d[256 + x * 8 + a : 257 + x * 8 + a, :] = row
        buf_sd[256 + x : 257 + x, :] = ng[base + 84 : base + 85, :]
    for a in range(8):
        buf_d[320 + a : 321 + a, :] = mass[a * 17 + 16 : a * 17 + 17, :]
    buf_sd[264:265, :] = mass[152:153, :]
    buf_sd[265:272, :] = jnp.zeros((7, 128), F32)


def brick_sums(bufs, first=0, count=1024):
    blocks = jnp.concatenate([buf[at : at + 128, :] for buf in bufs for at in (0, 128)], axis=1)
    target = blocks[125:126, :]
    bricks = lax.broadcasted_iota(jnp.int32, (count, blocks.shape[1]), 0).astype(F32) + float(first)
    hit = jnp.where(bricks == target, 1.0, 0.0).astype(BF16)
    return dot2(blocks, hit, NT)


def stepped(now, before, src, force, scale):
    return 2.0 * now - before + (src - force) * scale


def near_kernel(
    own, got_d, ng_low, ng, mass, fields, wave_old, adj_old, src, adj_src,
    near, edge, wave_next, adj_next, wave_buf, adj_buf, sem,
):
    keep_d = (lax.axis_index("depth") > 0).astype(F32)
    first = lax.broadcasted_iota(jnp.int32, (16, 128), 0) == 0

    def total(ch, a):
        if ch == 8:
            part = mass[a * 17 : a * 17 + 16, :]
        else:
            low, high = ch * NROW + a * 17, ch * NROW + (a - 4) * 17
            part = ng_low[low : low + 16, :] if a <= 4 else ng[high : high + 16, :]
            if a == 4:
                part = part + ng[high : high + 16, :]
        line = got_d[256 + ch * 8 + a : 257 + ch * 8 + a, :] * keep_d
        return part + jnp.where(first, line, 0.0)

    for ch in range(9):
        edge[ch] = total(ch, 0)
    for a in range(1, 8):
        scale = (DT * DT) / total(8, a)
        for t in range(4):
            at = slice(t * PLANE + a * 16, t * PLANE + a * 16 + 16)
            now = slice(t * COLUMN + a * 16, t * COLUMN + a * 16 + 16)
            adj = slice(now.start + 4 * COLUMN, now.stop + 4 * COLUMN)
            wave_buf[at, :] = stepped(fields[now, :], wave_old[at, :], src[at, :], total(t, a), scale)
            adj_buf[at, :] = stepped(
                fields[adj, :], adj_old[at, :], adj_src[at, :], total(4 + t, a), scale
            )
    copies = []
    for t in range(4):
        rows = pl.ds(t * PLANE + 16, PLANE - 16)
        for k, (buf, to) in enumerate(((wave_buf, wave_next), (adj_buf, adj_next))):
            copies.append(pltpu.make_async_copy(buf.at[rows], to.at[rows], sem.at[2 * t + k]))
    for c in copies:
        c.start()
    near[...] = brick_sums((own, got_d))
    for c in copies:
        c.wait()


def final_kernel(
    fields, wave_old, adj_old, src, adj_src, edge, near, got_s, got_sd, wave_in, adj_in,
    wave_next, adj_next, bricks, wave_buf, adj_buf, brick_buf, sem,
):
    keep_s = (lax.axis_index("surf") > 0).astype(F32)
    keep_d = (lax.axis_index("depth") > 0).astype(F32)
    first = lax.broadcasted_iota(jnp.int32, (16, 128), 0) == 0

    def total(ch):
        line = got_sd[256 + ch : 257 + ch, :] * (keep_s * keep_d)
        plane = got_s[256 + ch * 16 : 272 + ch * 16, :] * keep_s
        return edge[ch] + plane + jnp.where(first, line, 0.0)

    scale = (DT * DT) / total(8)
    copies = []
    for t in range(4):
        at = slice(t * PLANE, t * PLANE + 16)
        now = slice(t * COLUMN, t * COLUMN + 16)
        adj = slice(now.start + 4 * COLUMN, now.stop + 4 * COLUMN)
        wave_buf[t] = stepped(fields[now, :], wave_old[at, :], src[at, :], total(t), scale)
        adj_buf[t] = stepped(fields[adj, :], adj_old[at, :], adj_src[at, :], total(4 + t), scale)
        rows = pl.ds(t * PLANE, 16)
        for k, (buf, to) in enumerate(((wave_buf, wave_next), (adj_buf, adj_next))):
            copies.append(pltpu.make_async_copy(buf.at[t], to.at[rows], sem.at[2 * t + k]))
    for c in copies:
        c.start()
    for k in range(CHUNKS):
        cols = slice(k * (1024 // CHUNKS), (k + 1) * (1024 // CHUNKS))
        acc = near[:, cols] + brick_sums((got_s, got_sd), k * (1024 // CHUNKS), 1024 // CHUNKS)
        brick_buf[:, cols] = acc[0:125, :]
        copy = pltpu.make_async_copy(brick_buf.at[:, cols], bricks.at[:, cols], sem.at[8 + k])
        copy.start()
        copies.append(copy)
    for c in copies:
        c.wait()


def vmem(*shape):
    return pltpu.VMEM(shape, F32)


def out(*shape, dtype=F32):
    return jax.ShapeDtypeStruct(shape, dtype)


def send(x, ds, dd, wrap_s, wrap_d):
    ns, nd = lax.axis_size("surf"), lax.axis_size("depth")
    pairs = [
        (s * nd + d, (s + ds) % ns * nd + (d + dd) % nd)
        for s in range(ns)
        for d in range(nd)
        if (wrap_s or 0 <= s + ds < ns) and (wrap_d or 0 <= d + dd < nd)
    ]
    return lax.ppermute(x, ("surf", "depth"), pairs)


def call(kernel, name, ins, outs, scratch=(), specs=None, out_spaces=None, aliases=()):
    here = pl.BlockSpec(memory_space=pltpu.VMEM)
    spaces = out_spaces or [pltpu.VMEM] * len(outs)
    return pl.pallas_call(
        kernel,
        out_shape=tuple(outs),
        in_specs=specs or [here] * len(ins),
        out_specs=tuple(pl.BlockSpec(memory_space=space) for space in spaces),
        scratch_shapes=list(scratch),
        input_output_aliases=dict(aliases),
        compiler_params=pltpu.CompilerParams(vmem_limit_bytes=48 * 1024 * 1024),
        name=name,
    )(*ins)


def in_hbm(x):
    return pltpu.with_memory_space_constraint(x, pltpu.HBM)


def per_device(
    wave_now, wave_old, adj_now, adj_old, source, adj_source,
    inv_density, inv_modulus, element_cell, send_elem, send_brick, send_count,
):
    shape = wave_now.shape
    wave, wave_old, adj, adj_old, source, adj_source = (
        x.reshape(4 * PLANE, 128)
        for x in (wave_now, wave_old, adj_now, adj_old, source, adj_source)
    )
    there = pl.BlockSpec(memory_space=pltpu.HBM)
    line, plane = call(
        pack_kernel, "pack", [in_hbm(x) for x in (wave_now, adj_now)], (out(8, 8, 128), out(8, 16, 128)),
        [pltpu.SemaphoreType.DMA((4,))], [there] * 2,
    )
    hc = send(line, 0, -1, True, True)
    prep = call(
        prep_kernel,
        "prep",
        [in_hbm(x) for x in (wave, adj, inv_density, inv_modulus, element_cell, send_elem, send_brick, send_count)],
        (out(8 * COLUMN, 128), out(128, 256), out(160, 128), out(8, 256),
         out(512, 512, dtype=BF16), out(512, 512, dtype=BF16), out(128, 128)),
        [vmem(125, 256), vmem(125, 256), pltpu.VMEM((1, 256), jnp.int32),
         pltpu.VMEM((1, 4, 256), jnp.int32), pltpu.VMEM((1, 4, 256), jnp.int32),
         pltpu.SMEM((1, 4), jnp.int32), pltpu.SemaphoreType.DMA((14,)), vmem(160, 128), vmem(160, 128), vmem(64, 512)],
        [there] * 8,
    )
    hc, plane, prep = lax.optimization_barrier((hc, plane, tuple(prep)))
    fields, stiff, mass, targ, spread, fold, wcol = prep
    ha = send(jnp.concatenate([plane.reshape(128, 128), hc[:, 0]], 0), -1, 0, True, True)

    kern_low, ng_low, val_up, prod_up, frc_up = call(
        early_kernel,
        "early",
        (fields, hc.reshape(64, 128), stiff, spread, fold, wcol),
        (out(128, 128), out(8 * NROW, 128), out(160, 640), out(800, 128), out(160, 640)),
        [vmem(200, 512), vmem(200, 640), vmem(1000, 128), vmem(200, 640)],
    )
    ng, kern, buf_s = call(
        late_kernel,
        "late",
        (ha, stiff, spread, fold, wcol, kern_low, ng_low, mass, targ, val_up, prod_up, frc_up),
        (out(8 * NROW, 128), out(128, 128), out(400, 128)),
        [vmem(200, 512), vmem(40, 640),
         vmem(1000, 128), vmem(200, 640)],
    )
    got_s = send(buf_s, 1, 0, True, True)
    own, buf_d, buf_sd = call(
        pick_kernel,
        "pick",
        (kern_low, kern, ng_low, ng, mass, targ),
        (out(256, 128), out(328, 128), out(272, 128)),
    )
    got_d = send(buf_d, 0, 1, True, True)
    got_sd = send(buf_sd, 1, 1, False, False)
    field = out(4 * PLANE, 128)
    rest = (fields, wave_old, adj_old, source, adj_source)
    near, edge, wave_part, adj_part = call(
        near_kernel,
        "near",
        (own, got_d, ng_low, ng, mass) + rest,
        (out(128, 1024), out(9, 16, 128), field, field),
        [vmem(4 * PLANE, 128), vmem(4 * PLANE, 128), pltpu.SemaphoreType.DMA((8,))],
        out_spaces=[pltpu.VMEM, pltpu.VMEM, pltpu.HBM, pltpu.HBM],
    )
    wave_next, adj_next, bricks = call(
        final_kernel,
        "final",
        rest + (edge, near, got_s, got_sd, wave_part, adj_part),
        (field, field, out(125, 1024)),
        [vmem(4, 16, 128), vmem(4, 16, 128), vmem(125, 1024), pltpu.SemaphoreType.DMA((8 + CHUNKS,))],
        [pl.BlockSpec(memory_space=pltpu.VMEM)] * 9 + [there] * 2,
        [pltpu.HBM, pltpu.HBM, pl.ANY],
        ((9, 0), (10, 1)),
    )
    return wave_next.reshape(shape), adj_next.reshape(shape), bricks


def solution(mesh):
    field = P(None, "surf", "depth", None)
    both = ("surf", "depth")
    return jax.shard_map(
        per_device,
        mesh=mesh,
        in_specs=(field,) * 6
        + (P(None, both), P(None, both), P(both, None), P(both, None, None), P(both, None, None), P(both, None)),
        out_specs=(field, field, P(None, both)),
        check_vma=False,
    )
```
